512 devices in a mesh: dp: 128 (over z, y, core), shard: 4 (over x).
Axes of the slice: x: 4, y: 8, z: 8, core: 2. Of those that a mesh axis runs over, the one named last changes fastest.
Arguments:
- latent_grads: bfloat16 [128, 288, 2560], P('dp', None, 'shard'), may hold values from -132 to 132
- latent_errors: bfloat16 [128, 288, 2560], P('dp', None, 'shard'), may hold values from -3 to 3
- latent_moments: bfloat16 [288, 2560], P(None, 'shard'), may hold values from -2 to 2
- latent_coeffs: bfloat16 [2560, 32], P('shard'), may hold values from -5 to 5
- expand_grads: bfloat16 [128, 5120, 256], P('dp', 'shard'), may hold values from -132 to 132
- expand_errors: bfloat16 [128, 5120, 256], P('dp', 'shard'), may hold values from -3 to 3
- expand_moments: bfloat16 [5120, 256], P('shard'), may hold values from -2 to 2
- expand_coeffs: bfloat16 [256, 32], replicated, may hold values from -5 to 5
- gain_grads: bfloat16 [128, 256], P('dp'), may hold values from -132 to 132
- gain_moments: float32 [256], P('shard'), may hold values from -5 to 5
Outputs:
- latent_leftover: bfloat16 [128, 288, 2560], P('dp', None, 'shard')
- latent_momentum: bfloat16 [288, 2560], P(None, 'shard')
- latent_factor: bfloat16 [2560, 32], P('shard')
- expand_leftover: bfloat16 [128, 5120, 256], P('dp', 'shard')
- expand_momentum: bfloat16 [5120, 256], P('shard')
- expand_factor: bfloat16 [256, 32], replicated
- gain_momentum: float32 [256], P('shard')
The draws below stay inside these ranges and needn't reach their ends.
All inputs are finite; a program needn't handle non-finite values.
Results may differ from the reference program's by a relative error of at most 0.0044.
The reference program's roundings to bfloat16 on the way count: a program that leaves them out, or rounds other values in their place, can miss the bound.
Values may be sent and summed in bfloat16 or wider, within the bound.
No kernel may reach another device: no remote copies, remote signals or barrier semaphores. Data moves between devices by JAX's collectives and lax.ppermute only.
A program may use at most 64 MiB of HBM per device.

```python
import jax
import jax.numpy as jnp
from jax import lax

D = 2560
KV_RANK = 256
RANK = 32
NS_ITERS = 6
KVA_OUT = 288
KVB_OUT = 5120
N_DP = 128


def replica_draw(key, rows, columns, spike_dim):
    key_common, key_noise, key_order = jax.random.split(key, 3)
    common = jax.random.truncated_normal(key_common, -4.0, 4.0, (rows, columns), jnp.float32)
    noise = jax.random.truncated_normal(key_noise, -4.0, 4.0, (N_DP, rows, columns), jnp.float32)
    order = jax.random.permutation(key_order, N_DP).astype(jnp.int32)
    length = rows if spike_dim == 1 else columns
    position = lax.broadcasted_iota(jnp.int32, (N_DP, rows, columns), spike_dim)
    block = position * N_DP // length
    owner = order[:, None, None]
    factor = jnp.where(block == owner, 0.5 * N_DP, 1.0)
    return common[None] + 0.5 * factor * noise


def draw_latent_grads(key, part):
    return replica_draw(jax.random.fold_in(key, 11), KVA_OUT, D, 2).astype(jnp.bfloat16)


def draw_expand_grads(key, part):
    return replica_draw(jax.random.fold_in(key, 23), KVB_OUT, KV_RANK, 1).astype(jnp.bfloat16)


def draw_gain_grads(key, part):
    return replica_draw(jax.random.fold_in(key, 37), 1, KV_RANK, 2)[:, 0, :].astype(jnp.bfloat16)


def block_levels(key, shape, shards, least, largest):
    loudness = 1.0
    for dim, shards_of in shards:
        heights = jax.random.uniform(jax.random.fold_in(jax.random.fold_in(key, 6), dim), (shards_of,), jnp.float32, least / len(shards), largest / len(shards))
        loudness = loudness * jnp.repeat(jnp.exp(heights), shape[dim] // shards_of).reshape((-1,) + (1,) * (len(shape) - 1 - dim))
    return loudness


def gaussian(own_key, extent, deviation, reach, pieces=(), kind=jnp.bfloat16):
    gain = block_levels(own_key, extent, pieces, -0.22, 0.18) if pieces else 1.0
    entries = jax.random.normal(own_key, extent, jnp.float32) * deviation * gain
    return jnp.minimum(jnp.maximum(entries, -reach), reach).astype(kind)


def setup_inputs(seed: int = 0) -> dict:
    key_of = jax.random.split(jax.random.key(seed), 11)
    latent_grads = draw_latent_grads(jax.random.fold_in(key_of[10], 71), 0)
    latent_errors = gaussian(key_of[1], (N_DP, KVA_OUT, D), 0.5, 3.0, ((0, 128), (2, 4)))
    latent_moments = gaussian(key_of[2], (KVA_OUT, D), 0.3, 2.0, ((1, 4),))
    latent_coeffs = gaussian(key_of[3], (D, RANK), 1.0, 5.0, ((0, 4),))
    expand_grads = draw_expand_grads(jax.random.fold_in(key_of[10], 71), 0)
    expand_errors = gaussian(key_of[5], (N_DP, KVB_OUT, KV_RANK), 0.5, 3.0, ((0, 128), (1, 4)))
    expand_moments = gaussian(key_of[6], (KVB_OUT, KV_RANK), 0.3, 2.0, ((0, 4),))
    expand_coeffs = gaussian(key_of[7], (KV_RANK, RANK), 1.0, 5.0)
    gain_grads = draw_gain_grads(jax.random.fold_in(key_of[10], 71), 0)
    gain_moments = gaussian(key_of[9], (KV_RANK,), 1.0, 5.0, ((0, 4),), jnp.float32)
    return {"latent_grads": latent_grads, "latent_errors": latent_errors, "latent_moments": latent_moments, "latent_coeffs": latent_coeffs, "expand_grads": expand_grads, "expand_errors": expand_errors, "expand_moments": expand_moments, "expand_coeffs": expand_coeffs, "gain_grads": gain_grads, "gain_moments": gain_moments}


BETA = 0.9
EPSILON = 1e-06
HIGHEST = lax.Precision.HIGHEST

def inverse_root(gram_matrix):
    trace_sum = jnp.trace(gram_matrix) + EPSILON
    identity = jnp.eye(gram_matrix.shape[0], dtype=jnp.float32)
    root_left = gram_matrix / trace_sum
    root_right = identity
    for repeat_index in range(NS_ITERS):
        middle = 1.5 * identity - 0.5 * jnp.dot(root_right, root_left, precision=HIGHEST)
        root_left = jnp.dot(root_left, middle, precision=HIGHEST)
        root_right = jnp.dot(middle, root_right, precision=HIGHEST)
    return root_right / jnp.sqrt(trace_sum)

def compress(grads_all, errors_all, moments, coeffs):
    replicas = grads_all.shape[0]
    members = jnp.arange(replicas, dtype=jnp.int32)

    def merged_of(member):
        combined = grads_all[member].astype(jnp.float32) + errors_all[member].astype(jnp.float32)
        return combined.astype(jnp.bfloat16)

    def add_left(carry, member):
        return (carry + jnp.dot(merged_of(member), coeffs, preferred_element_type=jnp.float32), None)
    left_sum, unused = lax.scan(add_left, jnp.zeros((grads_all.shape[1], coeffs.shape[1]), jnp.float32), members)
    gram_matrix = jnp.dot(left_sum.T, left_sum, precision=HIGHEST)
    basis_rows = jnp.dot(left_sum, inverse_root(gram_matrix), precision=HIGHEST).astype(jnp.bfloat16)

    def add_right(carry, member):
        return (carry + jnp.dot(merged_of(member).T, basis_rows, preferred_element_type=jnp.float32), None)
    right_sum, unused = lax.scan(add_right, jnp.zeros((grads_all.shape[2], coeffs.shape[1]), jnp.float32), members)
    factor = (right_sum / replicas).astype(jnp.bfloat16)
    approx = jnp.dot(basis_rows, factor.T, preferred_element_type=jnp.float32)

    def leftover_of(member):
        combined = grads_all[member].astype(jnp.float32) + errors_all[member].astype(jnp.float32)
        return (combined - approx).astype(jnp.bfloat16)
    leftover = lax.map(leftover_of, members)
    momentum = (BETA * moments.astype(jnp.float32) + approx).astype(jnp.bfloat16)
    return (leftover, momentum, factor)

def reference(latent_grads, latent_errors, latent_moments, latent_coeffs, expand_grads, expand_errors, expand_moments, expand_coeffs, gain_grads, gain_moments):
    latent = compress(latent_grads, latent_errors, latent_moments, latent_coeffs)
    expand = compress(expand_grads, expand_errors, expand_moments, expand_coeffs)
    replicas = gain_grads.shape[0]
    gain_momentum = BETA * gain_moments + lax.optimization_barrier(jnp.sum(gain_grads.astype(jnp.float32), axis=0)) / replicas
    return (latent[0], latent[1], latent[2], expand[0], expand[1], expand[2], gain_momentum)
```

```python
import jax
import jax.numpy as jnp
from jax import lax
from jax.sharding import Mesh, PartitionSpec as P

NS_ITERS = 6
BETA = 0.9
EPSILON = 1e-06
HIGHEST = lax.Precision.HIGHEST
RANK = 32
RING = ("y", "core")
CROSS = ("z", "x")
DP = ("z", "y", "core")


def inverse_roots(grams):
    identity = jnp.eye(RANK, dtype=jnp.float32)
    trace_sum = jnp.sum(grams * identity, axis=(1, 2), keepdims=True) + EPSILON
    root_left = grams / trace_sum
    root_right = jnp.broadcast_to(identity, grams.shape)
    for repeat_index in range(NS_ITERS):
        middle = 1.5 * identity - 0.5 * jnp.matmul(root_right, root_left, precision=HIGHEST)
        root_left = jnp.matmul(root_left, middle, precision=HIGHEST)
        root_right = jnp.matmul(middle, root_right, precision=HIGHEST)
    return root_right / jnp.sqrt(trace_sum)


def spread(piece, axes, count):
    return lax.all_to_all(jnp.broadcast_to(piece, (count, *piece.shape)), axes, 0, 0)


def local(
    latent_grads,
    latent_errors,
    latent_moments,
    latent_coeffs,
    expand_grads,
    expand_errors,
    expand_moments,
    expand_coeffs,
    gain_grads,
    gain_moments,
):
    ring = lax.axis_size(RING)
    depth = lax.axis_size("z")
    shards = lax.axis_size("x")
    cross = depth * shards
    replicas = ring * depth
    shard = lax.axis_index("x")
    latent_rows, latent_cols = latent_grads.shape[1:]
    expand_rows, expand_cols = expand_grads.shape[1:]
    slab = expand_rows // ring
    latent_slabs = latent_rows // RANK
    owned = gain_moments.shape[0]
    gain_piece = owned * shards // ring

    latent_total = latent_grads[0].astype(jnp.float32) + latent_errors[0].astype(jnp.float32)
    latent_merged = latent_total.astype(jnp.bfloat16)
    expand_total = expand_grads[0].astype(jnp.float32) + expand_errors[0].astype(jnp.float32)
    expand_merged = expand_total.astype(jnp.bfloat16)

    expand_part = jnp.einsum(
        "pnk,kr->prn",
        expand_merged.reshape(ring, slab, expand_cols),
        expand_coeffs,
        preferred_element_type=jnp.float32,
    )
    latent_part = jnp.einsum(
        "pnk,kr->prn",
        latent_merged.reshape(latent_slabs, RANK, latent_cols),
        latent_coeffs,
        preferred_element_type=jnp.float32,
    )
    latent_part = jnp.pad(latent_part, ((0, ring - latent_slabs), (0, 0), (0, 0)))
    gain_part = gain_grads[0].astype(jnp.float32).reshape(ring, 1, gain_piece)
    gain_part = jnp.pad(gain_part, ((0, 0), (0, RANK - 1), (0, 0)))
    part = jnp.concatenate([expand_part, latent_part, gain_part], axis=2).astype(jnp.bfloat16)
    piece = lax.all_to_all(part, RING, 0, 0).astype(jnp.float32).sum(0)
    pieces = spread(piece.astype(jnp.bfloat16), CROSS, cross).astype(jnp.float32)
    pieces = pieces.reshape(depth, shards, RANK, -1).sum(0)
    expand_slabs = pieces[:, :, :slab]
    gram_part = jnp.einsum("xrn,xsn->rs", expand_slabs, expand_slabs, precision=HIGHEST)
    own = lax.dynamic_index_in_dim(pieces, shard, 0, keepdims=False)
    latent_slab = pieces[:, :, slab : slab + RANK].sum(0)
    mine = jnp.concatenate([own[:, :slab], latent_slab, own[:, slab + RANK :]], axis=1)
    width = mine.shape[1]
    mine = jnp.concatenate([mine, gram_part.reshape(-1, width)], axis=0)
    gathered = spread(mine, RING, ring)

    expand_left = gathered[:, :RANK, :slab]
    latent_left = gathered[:latent_slabs, :RANK, slab : slab + RANK]
    gain_summed = gathered[:, 0, slab + RANK :].reshape(-1)
    expand_gram = gathered[:, RANK:].sum(0).reshape(RANK, RANK)
    latent_gram = jnp.einsum("prn,psn->rs", latent_left, latent_left, precision=HIGHEST)
    roots = inverse_roots(jnp.stack([latent_gram, expand_gram]))
    latent_basis = jnp.einsum("prn,rs->spn", latent_left, roots[0], precision=HIGHEST)
    latent_basis = latent_basis.astype(jnp.bfloat16).reshape(RANK, latent_rows)
    expand_basis = jnp.einsum("prn,rs->spn", expand_left, roots[1], precision=HIGHEST)
    expand_basis = expand_basis.astype(jnp.bfloat16).reshape(RANK, expand_rows)

    latent_right = jnp.dot(latent_basis, latent_merged, preferred_element_type=jnp.float32)
    expand_right = jnp.dot(expand_basis, expand_merged, preferred_element_type=jnp.float32)
    right = jnp.concatenate([latent_right, expand_right], axis=1).astype(jnp.bfloat16)
    right = right.reshape(ring, RANK // ring, latent_cols + expand_cols)
    piece = lax.all_to_all(right, RING, 0, 0).astype(jnp.float32).sum(0)
    pieces = spread(piece.astype(jnp.bfloat16), CROSS, cross).astype(jnp.float32)
    pieces = pieces.reshape(depth, shards, RANK // ring, -1).sum(0)
    latent_right = lax.dynamic_index_in_dim(pieces, shard, 0, keepdims=False)[:, :latent_cols]
    expand_right = pieces[:, :, latent_cols:].sum(0)
    mine = jnp.concatenate([latent_right, expand_right], axis=1) / replicas
    factors = spread(mine.astype(jnp.bfloat16), RING, ring).reshape(RANK, -1)
    latent_factor = factors[:, :latent_cols]
    expand_factor = factors[:, latent_cols:]

    def finish(total, basis, factor, moments):
        approx = jnp.einsum("rn,rm->nm", basis, factor, preferred_element_type=jnp.float32)
        leftover = (total - approx).astype(jnp.bfloat16)[None]
        momentum = (BETA * moments.astype(jnp.float32) + approx).astype(jnp.bfloat16)
        return leftover, momentum, factor.T

    gain_summed = lax.dynamic_slice_in_dim(gain_summed, shard * owned, owned)
    gain_momentum = BETA * gain_moments + gain_summed / replicas
    return (
        *finish(latent_total, latent_basis, latent_factor, latent_moments),
        *finish(expand_total, expand_basis, expand_factor, expand_moments),
        gain_momentum,
    )


def solution(mesh):
    grid = Mesh(mesh.devices.reshape(8, 8, 2, 4), ("z", "y", "core", "x"))
    return jax.shard_map(
        local,
        mesh=grid,
        in_specs=(
            P(DP, None, "x"),
            P(DP, None, "x"),
            P(None, "x"),
            P("x", None),
            P(DP, "x", None),
            P(DP, "x", None),
            P("x", None),
            P(),
            P(DP, None),
            P("x"),
        ),
        out_specs=(
            P(DP, None, "x"),
            P(None, "x"),
            P("x", None),
            P(DP, "x", None),
            P("x", None),
            P(),
            P("x"),
        ),
        check_vma=False,
    )
```

```python
import functools

import jax
import jax.numpy as jnp
from jax import lax
from jax.experimental import pallas as pl
from jax.experimental.pallas import tpu as pltpu
from jax.sharding import Mesh, PartitionSpec as P

NS_ITERS = 6
BETA = 0.9
EPSILON = 1e-06
HIGHEST = lax.Precision.HIGHEST
RANK = 32
LANES = 128
RING = ("y", "core")
CROSS = ("z", "x")
DP = ("z", "y", "core")


def dot(left, right, left_dim, right_dim, precision=None):
    return lax.dot_general(
        left,
        right,
        (((left_dim,), (right_dim,)), ((), ())),
        precision=precision,
        preferred_element_type=jnp.float32,
    )


def inverse_roots(grams):
    row = lax.broadcasted_iota(jnp.int32, (RANK, RANK), 0)
    column = lax.broadcasted_iota(jnp.int32, (RANK, RANK), 1)
    identity = jnp.where(row == column, jnp.float32(1), jnp.float32(0))
    traces = [jnp.sum(g * identity, keepdims=True) + EPSILON for g in grams]
    lefts = [g / t for g, t in zip(grams, traces)]
    middles = [1.5 * identity - 0.5 * y for y in lefts]
    rights = middles
    for repeat_index in range(1, NS_ITERS):
        lefts = [dot(y, m, 1, 0, HIGHEST) for y, m in zip(lefts, middles)]
        middles = [
            1.5 * identity - 0.5 * dot(z, y, 1, 0, HIGHEST) for z, y in zip(rights, lefts)
        ]
        rights = [dot(m, z, 1, 0, HIGHEST) for m, z in zip(middles, rights)]
    return [z / jnp.sqrt(t) for z, t in zip(rights, traces)]


def add(left, right):
    return left.astype(jnp.float32) + right.astype(jnp.float32)


def left_kernel(lg, le, lc, eg, ee, ec, part, lm, em):
    ring = part.shape[0]
    lm[...] = add(lg[0], le[0]).astype(jnp.bfloat16)
    em[...] = add(eg[0], ee[0]).astype(jnp.bfloat16)
    slab = em.shape[0] // ring
    latent_slab = lm.shape[0] // ring
    latent = dot(lc[...], lm[...], 1, 1)
    rest = jnp.zeros((RANK, LANES - slab - latent_slab), jnp.float32)
    for p in range(ring):
        expand = dot(ec[...], em[pl.ds(p * slab, slab), :], 1, 1)
        own = latent[:, p * latent_slab : (p + 1) * latent_slab]
        part[p] = jnp.concatenate([expand, own, rest], axis=1).astype(jnp.bfloat16)


def total(parts):
    whole = parts[0].astype(jnp.float32)
    for p in range(1, parts.shape[0]):
        whole = whole + parts[p].astype(jnp.float32)
    return whole


def sum_kernel(parts, out):
    piece = total(parts).astype(out.dtype)
    for p in range(out.shape[0]):
        out[p] = piece


def gram_kernel(slab, latent_slab, shard, pieces, out):
    depth, shards = pieces.shape[:2]
    half = RANK // 2
    gram = jnp.zeros((RANK, RANK), jnp.float32)
    every = jnp.zeros((RANK, LANES), jnp.float32)
    own = jnp.zeros((RANK, LANES), jnp.float32)
    for x in range(shards):
        piece = total(pieces.at[:, x])
        expand = piece[:, :slab]
        gram = gram + dot(expand, expand, 1, 1, HIGHEST)
        every = every + piece
        own = jnp.where(shard[0] == x, piece, own)
    lower = gram[half:, half:]
    corner = jnp.concatenate([lower[:, : half // 2], lower[:, half // 2 :]], axis=0)
    used = slab + latent_slab
    rest = jnp.zeros((RANK, LANES - used - half - half // 2), jnp.float32)
    mine = jnp.concatenate(
        [own[:, :slab], every[:, slab:used], gram[:, :half], corner, rest], axis=1
    )
    for p in range(out.shape[0]):
        out[p] = mine


def right_kernel(gathered, lm, em, gain, right, lb, eb):
    ring = gathered.shape[0]
    slab = em.shape[0] // ring
    used = slab + lm.shape[0] // ring
    half = RANK // 2
    left = jnp.concatenate([gathered[p, :, slab:used] for p in range(ring)], axis=1)
    latent_gram = dot(left, left, 1, 1, HIGHEST)
    packed = total(gathered)
    first = packed[:, used : used + half]
    corner = packed[:, used + half : used + half + half // 2]
    corner = jnp.concatenate([corner[:half], corner[half:]], axis=1)
    second = jnp.concatenate([first[half:].T, corner], axis=0)
    expand_gram = jnp.concatenate([first, second], axis=1)
    latent_root, expand_root = inverse_roots([latent_gram, expand_gram])
    lb[...] = dot(latent_root, left, 0, 0, HIGHEST).astype(jnp.bfloat16)
    left = jnp.concatenate([gathered[p, :, :slab] for p in range(ring)], axis=1)
    eb[...] = dot(expand_root, left, 0, 0, HIGHEST).astype(jnp.bfloat16)
    tiles = [
        dot(lb[...], lm[...], 1, 0).astype(jnp.bfloat16),
        dot(eb[...], em[...], 1, 0).astype(jnp.bfloat16),
    ]
    p = 0
    for rows in range(0, RANK, half):
        for tile in tiles:
            for at in range(0, tile.shape[1], LANES):
                right[p] = tile[rows : rows + half, at : at + LANES]
                p += 1
    gains = [gain[:, at : at + LANES].astype(jnp.float32) for at in range(0, gain.shape[1], LANES)]
    gains.append(jnp.zeros((half - len(gains), LANES), jnp.float32))
    right[p] = jnp.concatenate(gains, axis=0).astype(jnp.bfloat16)
    for p in range(p + 1, ring):
        right[p] = jnp.zeros(right.shape[1:], right.dtype)


def halves(whole, is_gain):
    high = whole.astype(jnp.bfloat16).astype(jnp.float32)
    low = whole - high
    row = lax.broadcasted_iota(jnp.int32, whole.shape, 0)
    low = jnp.concatenate([low[:2], low[:2], low[4:]], axis=0)
    spare = jnp.logical_and(is_gain, jnp.logical_and(row >= 2, row < 4))
    return jnp.where(spare, low, high).astype(jnp.bfloat16)


def right_sum_kernel(gain_tile, ring, parts, out):
    piece = halves(total(parts), ring[0] == gain_tile)
    for p in range(out.shape[0]):
        out[p] = piece


def factor_kernel(gain_tile, latent_tiles, tiles, replicas, ring, shard, pieces, out):
    depth, shards = pieces.shape[:2]
    is_gain = ring[0] == gain_tile
    crossed = jnp.logical_and(ring[0] < gain_tile, lax.rem(ring[0], tiles) >= latent_tiles)
    whole = jnp.zeros(pieces.shape[2:], jnp.float32)
    for x in range(shards):
        piece = total(pieces.at[:, x])
        whole = whole + jnp.where(jnp.logical_or(crossed, shard[0] == x), piece, 0.0)
    whole = whole / replicas
    joined = jnp.concatenate([whole[:2] + whole[2:4], whole[2:]], axis=0)
    piece = halves(jnp.where(is_gain, joined, whole), is_gain)
    for p in range(out.shape[0]):
        out[p] = piece


def finish_kernel(shard, factors, lb, lg, le, lv, eb, eg, ee, ev, gv, *outs):
    ll, lmom, lf, el, emom, ef, gmom = outs
    half = RANK // 2
    tiles = (lf.shape[1] + ef.shape[1]) // LANES
    first = 0
    for basis, grads, errors, moments, leftover, momentum, out in (
        (lb, lg, le, lv, ll, lmom, lf),
        (eb, eg, ee, ev, el, emom, ef),
    ):
        count = out.shape[1] // LANES
        for t in range(count):
            for upper in range(2):
                out[half * upper : half * (upper + 1), LANES * t : LANES * (t + 1)] = factors[
                    upper * tiles + first + t
                ]
        first += count
        approx = dot(basis[...], out[...], 0, 0)
        leftover[0] = (add(grads[0], errors[0]) - approx).astype(jnp.bfloat16)
        momentum[...] = (BETA * moments[...].astype(jnp.float32) + approx).astype(jnp.bfloat16)
    gain = factors[2 * tiles].astype(jnp.float32)
    gain = gain[:2] + gain[2:4]
    owned = gv.shape[1]
    mean = jnp.zeros((1, owned), jnp.float32)
    for x in range(2 * LANES // owned):
        at = x * owned
        own = gain[at // LANES : at // LANES + 1, at % LANES : at % LANES + owned]
        mean = jnp.where(shard[0] == x, own, mean)
    gmom[...] = BETA * gv[...] + mean


def call(kernel, name, outs, args, scalars=0, fast_in=()):
    specs = [pl.BlockSpec(memory_space=pltpu.SMEM)] * scalars
    specs += [pl.BlockSpec(memory_space=pltpu.VMEM)] * (len(args) - scalars)
    args = [
        pltpu.with_memory_space_constraint(a, pltpu.VMEM) if i in fast_in else a
        for i, a in enumerate(args)
    ]
    shapes = [
        pltpu.VMEM(shape, dtype) if fast else jax.ShapeDtypeStruct(shape, dtype)
        for shape, dtype, fast in outs
    ]
    return pl.pallas_call(
        kernel,
        out_shape=shapes,
        in_specs=specs,
        out_specs=[pl.BlockSpec(memory_space=pltpu.VMEM)] * len(shapes),
        name=name,
    )(*args)


def exchange(array, axes):
    return lax.all_to_all(array, axes, 0, 0)


def local(
    latent_grads,
    latent_errors,
    latent_moments,
    latent_coeffs,
    expand_grads,
    expand_errors,
    expand_moments,
    expand_coeffs,
    gain_grads,
    gain_moments,
):
    ring = lax.axis_size(RING)
    depth = lax.axis_size("z")
    shards = lax.axis_size("x")
    cross = depth * shards
    shard = lax.axis_index("x").astype(jnp.int32).reshape(1)
    place = lax.axis_index(RING).astype(jnp.int32).reshape(1)
    latent_rows, latent_cols = latent_grads.shape[1:]
    expand_rows, expand_cols = expand_grads.shape[1:]
    slab = expand_rows // ring
    latent_slab = latent_rows // ring
    latent_tiles = latent_cols // LANES
    tiles = latent_tiles + expand_cols // LANES
    half = RANK // 2
    bf16, f32 = jnp.bfloat16, jnp.float32

    part, latent_merged, expand_merged = call(
        left_kernel,
        "left",
        (
            ((ring, RANK, LANES), bf16, True),
            ((latent_rows, latent_cols), bf16, True),
            ((expand_rows, expand_cols), bf16, True),
        ),
        (
            latent_grads,
            latent_errors,
            latent_coeffs.T,
            expand_grads,
            expand_errors,
            expand_coeffs.T,
        ),
    )
    part, shard, place = lax.optimization_barrier((part, shard, place))
    part = exchange(part, RING)
    (piece,) = call(sum_kernel, "left_sum", (((cross, RANK, LANES), bf16, True),), (part,), 0, (0,))
    pieces = exchange(piece, CROSS).reshape(depth, shards, RANK, LANES)
    (mine,) = call(
        functools.partial(gram_kernel, slab, latent_slab),
        "gram",
        (((ring, RANK, LANES), f32, True),),
        (shard, pieces),
        1,
        (1,),
    )
    gathered = exchange(mine, RING)
    right, latent_basis, expand_basis = call(
        right_kernel,
        "right",
        (
            ((ring, half, LANES), bf16, True),
            ((RANK, latent_rows), bf16, True),
            ((RANK, expand_rows), bf16, True),
        ),
        (gathered, latent_merged, expand_merged, gain_grads),
        0,
        (0, 1, 2),
    )
    right = exchange(right, RING)
    (piece,) = call(
        functools.partial(right_sum_kernel, 2 * tiles),
        "right_sum",
        (((cross, half, LANES), bf16, True),),
        (place, right),
        1,
        (1,),
    )
    pieces = exchange(piece, CROSS).reshape(depth, shards, half, LANES)
    (mine,) = call(
        functools.partial(factor_kernel, 2 * tiles, latent_tiles, tiles, ring * depth),
        "factor",
        (((ring, half, LANES), bf16, True),),
        (place, shard, pieces),
        2,
        (2,),
    )
    factors = exchange(mine, RING)
    outs = call(
        finish_kernel,
        "finish",
        (
            ((1, latent_rows, latent_cols), bf16, False),
            ((latent_rows, latent_cols), bf16, False),
            ((RANK, latent_cols), bf16, False),
            ((1, expand_rows, expand_cols), bf16, False),
            ((expand_rows, expand_cols), bf16, False),
            ((RANK, expand_cols), bf16, False),
            ((1, gain_moments.shape[0]), f32, False),
        ),
        (
            shard,
            factors,
            latent_basis,
            latent_grads,
            latent_errors,
            latent_moments,
            expand_basis,
            expand_grads,
            expand_errors,
            expand_moments,
            gain_moments.reshape(1, -1),
        ),
        1,
        (1, 2, 6),
    )
    return (*outs[:2], outs[2].T, *outs[3:5], outs[5].T, outs[6].reshape(-1))


def solution(mesh):
    grid = Mesh(mesh.devices.reshape(8, 8, 2, 4), ("z", "y", "core", "x"))
    return jax.shard_map(
        local,
        mesh=grid,
        in_specs=(
            P(DP, None, "x"),
            P(DP, None, "x"),
            P(None, "x"),
            P("x", None),
            P(DP, "x", None),
            P(DP, "x", None),
            P("x", None),
            P(),
            P(DP, None),
            P("x"),
        ),
        out_specs=(
            P(DP, None, "x"),
            P(None, "x"),
            P("x", None),
            P(DP, "x", None),
            P("x", None),
            P(),
            P("x"),
        ),
        check_vma=False,
    )
```

```python
import functools

import jax
import jax.numpy as jnp
from jax import lax
from jax.experimental import pallas as pl
from jax.experimental.pallas import tpu as pltpu
from jax.sharding import Mesh, PartitionSpec as P

NS_ITERS = 6
BETA = 0.9
EPSILON = 1e-06
HIGHEST = lax.Precision.HIGHEST
RANK = 32
LANES = 128
EXPAND_CUTS = (0, 256, 512, 768, 1024, 1280)
LATENT_CUTS = (0, 128, 288)
RING = ("y", "core")
CROSS = ("z", "x")
DP = ("z", "y", "core")


def dot(left, right, left_dim, right_dim, precision=None):
    return lax.dot_general(
        left,
        right,
        (((left_dim,), (right_dim,)), ((), ())),
        precision=precision,
        preferred_element_type=jnp.float32,
    )


def inverse_roots(grams):
    row = lax.broadcasted_iota(jnp.int32, (RANK, RANK), 0)
    column = lax.broadcasted_iota(jnp.int32, (RANK, RANK), 1)
    identity = jnp.where(row == column, jnp.float32(1), jnp.float32(0))
    traces = [jnp.sum(g * identity, keepdims=True) + EPSILON for g in grams]
    lefts = [g / t for g, t in zip(grams, traces)]
    middles = [1.5 * identity - 0.5 * y for y in lefts]
    rights = middles
    for repeat_index in range(1, NS_ITERS):
        lefts = [dot(y, m, 1, 0, HIGHEST) for y, m in zip(lefts, middles)]
        middles = [
            1.5 * identity - 0.5 * dot(z, y, 1, 0, HIGHEST) for z, y in zip(rights, lefts)
        ]
        rights = [dot(m, z, 1, 0, HIGHEST) for m, z in zip(middles, rights)]
    return [z / jnp.sqrt(t) for z, t in zip(rights, traces)]


def add(left, right):
    return left.astype(jnp.float32) + right.astype(jnp.float32)


def left_kernel(lg, le, lc, eg, ee, ec, part, lm, em, lgv, lev, lcv, egv, eev, ecv, sems):
    ring = part.shape[0]
    slab = em.shape[0] // ring
    latent_slab = lm.shape[0] // ring
    copies = []

    def fetch(source, target):
        copies.append(pltpu.make_async_copy(source, target, sems.at[len(copies)]))
        copies[-1].start()

    fetch(lc, lcv)
    fetch(lg.at[0], lgv)
    fetch(le.at[0], lev)
    fetch(ec, ecv)
    fetch(eg.at[0], egv)
    fetch(ee.at[0], eev)
    for c in range(3):
        copies[c].wait()
    lm[...] = add(lgv[...], lev[...]).astype(jnp.bfloat16)
    latent = dot(lcv[...], lm[...], 1, 1)
    rest = jnp.zeros((RANK, LANES - slab - latent_slab), jnp.float32)
    for copy in copies[3:]:
        copy.wait()
    em[...] = add(egv[...], eev[...]).astype(jnp.bfloat16)
    for p in range(ring):
        expand = dot(ecv[...], em[pl.ds(p * slab, slab), :], 1, 1)
        own = latent[:, p * latent_slab : (p + 1) * latent_slab]
        part[p] = jnp.concatenate([expand, own, rest], axis=1).astype(jnp.bfloat16)


def total(parts):
    whole = parts[0].astype(jnp.float32)
    for p in range(1, parts.shape[0]):
        whole = whole + parts[p].astype(jnp.float32)
    return whole


def sum_kernel(parts, out):
    piece = total(parts).astype(out.dtype)
    for p in range(out.shape[0]):
        out[p] = piece


def gram_kernel(slab, latent_slab, shard, pieces, out):
    depth, shards = pieces.shape[:2]
    half = RANK // 2
    gram = jnp.zeros((RANK, RANK), jnp.float32)
    every = jnp.zeros((RANK, LANES), jnp.float32)
    own = jnp.zeros((RANK, LANES), jnp.float32)
    for x in range(shards):
        piece = total(pieces.at[:, x])
        expand = piece[:, :slab]
        gram = gram + dot(expand, expand, 1, 1, HIGHEST)
        every = every + piece
        own = jnp.where(shard[0] == x, piece, own)
    lower = gram[half:, half:]
    corner = jnp.concatenate([lower[:, : half // 2], lower[:, half // 2 :]], axis=0)
    used = slab + latent_slab
    rest = jnp.zeros((RANK, LANES - used - half - half // 2), jnp.float32)
    mine = jnp.concatenate(
        [own[:, :slab], every[:, slab:used], gram[:, :half], corner, rest], axis=1
    )
    for p in range(out.shape[0]):
        out[p] = mine


def right_kernel(gathered, lm, em, gain, right, lb, eb):
    ring = gathered.shape[0]
    slab = em.shape[0] // ring
    used = slab + lm.shape[0] // ring
    half = RANK // 2
    left = jnp.concatenate([gathered[p, :, slab:used] for p in range(ring)], axis=1)
    latent_gram = dot(left, left, 1, 1, HIGHEST)
    packed = total(gathered)
    first = packed[:, used : used + half]
    corner = packed[:, used + half : used + half + half // 2]
    corner = jnp.concatenate([corner[:half], corner[half:]], axis=1)
    second = jnp.concatenate([first[half:].T, corner], axis=0)
    expand_gram = jnp.concatenate([first, second], axis=1)
    latent_root, expand_root = inverse_roots([latent_gram, expand_gram])
    lb[...] = dot(latent_root, left, 0, 0, HIGHEST).astype(jnp.bfloat16)
    left = jnp.concatenate([gathered[p, :, :slab] for p in range(ring)], axis=1)
    eb[...] = dot(expand_root, left, 0, 0, HIGHEST).astype(jnp.bfloat16)
    tiles = [
        dot(lb[...], lm[...], 1, 0).astype(jnp.bfloat16),
        dot(eb[...], em[...], 1, 0).astype(jnp.bfloat16),
    ]
    p = 0
    for rows in range(0, RANK, half):
        for tile in tiles:
            for at in range(0, tile.shape[1], LANES):
                right[p] = tile[rows : rows + half, at : at + LANES]
                p += 1
    gains = [gain[:, at : at + LANES].astype(jnp.float32) for at in range(0, gain.shape[1], LANES)]
    gains.append(jnp.zeros((half - len(gains), LANES), jnp.float32))
    right[p] = jnp.concatenate(gains, axis=0).astype(jnp.bfloat16)
    for p in range(p + 1, ring):
        right[p] = jnp.zeros(right.shape[1:], right.dtype)


def halves(whole, is_gain):
    high = whole.astype(jnp.bfloat16).astype(jnp.float32)
    low = whole - high
    row = lax.broadcasted_iota(jnp.int32, whole.shape, 0)
    low = jnp.concatenate([low[:2], low[:2], low[4:]], axis=0)
    spare = jnp.logical_and(is_gain, jnp.logical_and(row >= 2, row < 4))
    return jnp.where(spare, low, high).astype(jnp.bfloat16)


def right_sum_kernel(gain_tile, ring, parts, out):
    piece = halves(total(parts), ring[0] == gain_tile)
    for p in range(out.shape[0]):
        out[p] = piece


def factor_kernel(gain_tile, latent_tiles, tiles, replicas, ring, shard, pieces, out):
    depth, shards = pieces.shape[:2]
    is_gain = ring[0] == gain_tile
    crossed = jnp.logical_and(ring[0] < gain_tile, lax.rem(ring[0], tiles) >= latent_tiles)
    whole = jnp.zeros(pieces.shape[2:], jnp.float32)
    for x in range(shards):
        piece = total(pieces.at[:, x])
        whole = whole + jnp.where(jnp.logical_or(crossed, shard[0] == x), piece, 0.0)
    whole = whole / replicas
    joined = jnp.concatenate([whole[:2] + whole[2:4], whole[2:]], axis=0)
    piece = halves(jnp.where(is_gain, joined, whole), is_gain)
    for p in range(out.shape[0]):
        out[p] = piece


def finish_kernel(shard, factors, lb, lg, le, lv, eb, eg, ee, ev, gv, *refs):
    ll, lmom, lf, el, emom, ef, gmom = refs[:7]
    llv, lmv, lfv, elv, emv, efv, gmv, sems = refs[7:]
    half = RANK // 2
    tiles = (lf.shape[1] + ef.shape[1]) // LANES
    copies = []

    def send(source, target):
        copies.append(pltpu.make_async_copy(source, target, sems.at[len(copies)]))
        copies[-1].start()

    first = 0
    for factor, out in ((lfv, lf), (efv, ef)):
        count = factor.shape[1] // LANES
        for t in range(count):
            for upper in range(2):
                factor[half * upper : half * (upper + 1), LANES * t : LANES * (t + 1)] = factors[
                    upper * tiles + first + t
                ]
        first += count
        send(factor, out)
    for basis, factor, grads, errors, moments, kept, leftover, fresh, momentum, cuts in (
        (eb, efv, eg, ee, ev, elv, el, emv, emom, EXPAND_CUTS),
        (lb, lfv, lg, le, lv, llv, ll, lmv, lmom, LATENT_CUTS),
    ):
        for low, high in zip(cuts, cuts[1:]):
            rows = pl.ds(low, high - low)
            approx = dot(basis[:, low:high], factor[...], 0, 0)
            whole = add(grads[0, rows, :], errors[0, rows, :])
            kept[rows, :] = (whole - approx).astype(jnp.bfloat16)
            send(kept.at[rows], leftover.at[0, rows])
            fresh[rows, :] = (BETA * moments[rows, :].astype(jnp.float32) + approx).astype(jnp.bfloat16)
            send(fresh.at[rows], momentum.at[rows])
    gain = factors[2 * tiles].astype(jnp.float32)
    gain = gain[:2] + gain[2:4]
    owned = gv.shape[1]
    mean = jnp.zeros((1, owned), jnp.float32)
    for x in range(2 * LANES // owned):
        at = x * owned
        own = gain[at // LANES : at // LANES + 1, at % LANES : at % LANES + owned]
        mean = jnp.where(shard[0] == x, own, mean)
    gmv[...] = BETA * gv[...] + mean
    send(gmv, gmom)
    for copy in copies:
        copy.wait()


def call(kernel, name, outs, args, scalars=0, fast=(), slow=(), scratch=()):
    args = list(args)
    specs = [pl.BlockSpec(memory_space=pltpu.SMEM)] * scalars
    for i in range(scalars, len(args)):
        space = pltpu.HBM if i in slow else pltpu.VMEM
        specs.append(pl.BlockSpec(memory_space=space))
        if i in slow or i in fast:
            args[i] = pltpu.with_memory_space_constraint(args[i], space)
    shapes = [
        pltpu.VMEM(shape, dtype) if near else jax.ShapeDtypeStruct(shape, dtype)
        for shape, dtype, near in outs
    ]
    return pl.pallas_call(
        kernel,
        out_shape=shapes,
        in_specs=specs,
        out_specs=[pl.BlockSpec(memory_space=pltpu.VMEM if near else pl.ANY) for *_, near in outs],
        scratch_shapes=scratch,
        compiler_params=pltpu.CompilerParams(vmem_limit_bytes=16 << 20),
        name=name,
    )(*args)


def exchange(array, axes):
    return lax.all_to_all(array, axes, 0, 0)


def local(
    latent_grads,
    latent_errors,
    latent_moments,
    latent_coeffs,
    expand_grads,
    expand_errors,
    expand_moments,
    expand_coeffs,
    gain_grads,
    gain_moments,
):
    ring = lax.axis_size(RING)
    depth = lax.axis_size("z")
    shards = lax.axis_size("x")
    cross = depth * shards
    shard = lax.axis_index("x").astype(jnp.int32).reshape(1)
    place = lax.axis_index(RING).astype(jnp.int32).reshape(1)
    latent_rows, latent_cols = latent_grads.shape[1:]
    expand_rows, expand_cols = expand_grads.shape[1:]
    slab = expand_rows // ring
    latent_slab = latent_rows // ring
    latent_tiles = latent_cols // LANES
    tiles = latent_tiles + expand_cols // LANES
    half = RANK // 2
    bf16, f32 = jnp.bfloat16, jnp.float32

    latent_shape, expand_shape = (latent_rows, latent_cols), (expand_rows, expand_cols)
    part, latent_merged, expand_merged = call(
        left_kernel,
        "left",
        (
            ((ring, RANK, LANES), bf16, True),
            (latent_shape, bf16, True),
            (expand_shape, bf16, True),
        ),
        (
            latent_grads,
            latent_errors,
            latent_coeffs.T,
            expand_grads,
            expand_errors,
            expand_coeffs.T,
        ),
        slow=range(6),
        scratch=(
            pltpu.VMEM(latent_shape, bf16),
            pltpu.VMEM(latent_shape, bf16),
            pltpu.VMEM((RANK, latent_cols), bf16),
            pltpu.VMEM(expand_shape, bf16),
            pltpu.VMEM(expand_shape, bf16),
            pltpu.VMEM((RANK, expand_cols), bf16),
            pltpu.SemaphoreType.DMA((6,)),
        ),
    )
    part, shard, place = lax.optimization_barrier((part, shard, place))
    part = exchange(part, RING)
    (piece,) = call(sum_kernel, "left_sum", (((cross, RANK, LANES), bf16, True),), (part,), 0, (0,))
    pieces = exchange(piece, CROSS).reshape(depth, shards, RANK, LANES)
    (mine,) = call(
        functools.partial(gram_kernel, slab, latent_slab),
        "gram",
        (((ring, RANK, LANES), f32, True),),
        (shard, pieces),
        1,
        (1,),
    )
    gathered = exchange(mine, RING)
    right, latent_basis, expand_basis = call(
        right_kernel,
        "right",
        (
            ((ring, half, LANES), bf16, True),
            ((RANK, latent_rows), bf16, True),
            ((RANK, expand_rows), bf16, True),
        ),
        (gathered, latent_merged, expand_merged, gain_grads),
        0,
        (0, 1, 2),
    )
    right = exchange(right, RING)
    (piece,) = call(
        functools.partial(right_sum_kernel, 2 * tiles),
        "right_sum",
        (((cross, half, LANES), bf16, True),),
        (place, right),
        1,
        (1,),
    )
    pieces = exchange(piece, CROSS).reshape(depth, shards, half, LANES)
    (mine,) = call(
        functools.partial(factor_kernel, 2 * tiles, latent_tiles, tiles, ring * depth),
        "factor",
        (((ring, half, LANES), bf16, True),),
        (place, shard, pieces),
        2,
        (2,),
    )
    factors = exchange(mine, RING)
    owned = (1, gain_moments.shape[0])
    latent_factor, expand_factor = (RANK, latent_cols), (RANK, expand_cols)
    outs = call(
        finish_kernel,
        "finish",
        (
            ((1, *latent_shape), bf16, False),
            (latent_shape, bf16, False),
            (latent_factor, bf16, False),
            ((1, *expand_shape), bf16, False),
            (expand_shape, bf16, False),
            (expand_factor, bf16, False),
            (owned, f32, False),
        ),
        (
            shard,
            factors,
            latent_basis,
            latent_grads,
            latent_errors,
            latent_moments,
            expand_basis,
            expand_grads,
            expand_errors,
            expand_moments,
            gain_moments.reshape(1, -1),
        ),
        scalars=1,
        fast=range(1, 11),
        scratch=(
            pltpu.VMEM(latent_shape, bf16),
            pltpu.VMEM(latent_shape, bf16),
            pltpu.VMEM(latent_factor, bf16),
            pltpu.VMEM(expand_shape, bf16),
            pltpu.VMEM(expand_shape, bf16),
            pltpu.VMEM(expand_factor, bf16),
            pltpu.VMEM(owned, f32),
            pltpu.SemaphoreType.DMA((3 + 2 * (len(EXPAND_CUTS) + len(LATENT_CUTS) - 2),)),
        ),
    )
    return (*outs[:2], outs[2].T, *outs[3:5], outs[5].T, outs[6].reshape(-1))


def solution(mesh):
    grid = Mesh(mesh.devices.reshape(8, 8, 2, 4), ("z", "y", "core", "x"))
    return jax.shard_map(
        local,
        mesh=grid,
        in_specs=(
            P(DP, None, "x"),
            P(DP, None, "x"),
            P(None, "x"),
            P("x", None),
            P(DP, "x", None),
            P(DP, "x", None),
            P("x", None),
            P(),
            P(DP, None),
            P("x"),
        ),
        out_specs=(
            P(DP, None, "x"),
            P(None, "x"),
            P("x", None),
            P(DP, "x", None),
            P("x", None),
            P(),
            P("x"),
        ),
        check_vma=False,
    )
```

```python
import functools

import jax
import jax.numpy as jnp
from jax import lax
from jax.experimental import pallas as pl
from jax.experimental.pallas import tpu as pltpu
from jax.sharding import Mesh, PartitionSpec as P

NS_ITERS = 6
BETA = 0.9
EPSILON = 1e-06
RANK = 32
LANES = 128
EXPAND_CUTS = (0, 256, 512, 768, 1024, 1280)
LATENT_CUTS = (0, 128, 288)
RING = ("core", "y")
CROSS = ("x", "z")
DP = ("z", "y", "core")


def dot(left, right, left_dim, right_dim):
    dims = (((left_dim,), (right_dim,)), ((), ()))
    return lax.dot_general(left, right, dims, preferred_element_type=jnp.float32)


def split(whole):
    high = whole.astype(jnp.bfloat16)
    return high, (whole - high.astype(jnp.float32)).astype(jnp.bfloat16)


def fine_dot(left, right, left_dim, right_dim):
    (lh, ll), (rh, rl) = split(left), split(right)
    small = dot(lh, rl, left_dim, right_dim) + dot(ll, rh, left_dim, right_dim)
    return dot(lh, rh, left_dim, right_dim) + small


def inverse_roots(grams):
    row = lax.broadcasted_iota(jnp.int32, (RANK, RANK), 0)
    column = lax.broadcasted_iota(jnp.int32, (RANK, RANK), 1)
    identity = jnp.where(row == column, jnp.float32(1), jnp.float32(0))
    traces = [jnp.sum(g * identity, keepdims=True) + EPSILON for g in grams]
    lefts = [g / t for g, t in zip(grams, traces)]
    middles = [1.5 * identity - 0.5 * y for y in lefts]
    rights = middles
    for repeat_index in range(1, NS_ITERS):
        lefts = [fine_dot(y, m, 1, 0) for y, m in zip(lefts, middles)]
        middles = [
            1.5 * identity - 0.5 * fine_dot(z, y, 1, 0) for z, y in zip(rights, lefts)
        ]
        rights = [fine_dot(m, z, 1, 0) for m, z in zip(middles, rights)]
    return [z / jnp.sqrt(t) for z, t in zip(rights, traces)]


def add(left, right):
    return left.astype(jnp.float32) + right.astype(jnp.float32)


def left_kernel(lg, le, lc, eg, ee, ec, gg, gm, part, lm, em, ggv, gmv, lgv, lev, lcv, egv, eev, ecv, sems):
    ring = part.shape[0]
    slab = em.shape[0] // ring
    latent_slab = lm.shape[0] // ring
    copies = []

    def fetch(source, target):
        copies.append(pltpu.make_async_copy(source, target, sems.at[len(copies)]))
        copies[-1].start()

    fetch(lc, lcv)
    fetch(lg.at[0], lgv)
    fetch(le.at[0], lev)
    fetch(ec, ecv)
    fetch(eg.at[0], egv)
    fetch(ee.at[0], eev)
    fetch(gg, ggv)
    fetch(gm, gmv)
    for c in range(3):
        copies[c].wait()
    lm[...] = add(lgv[...], lev[...]).astype(jnp.bfloat16)
    latent = dot(lcv[...], lm[...], 1, 1)
    rest = jnp.zeros((RANK, LANES - slab - latent_slab), jnp.float32)
    for copy in copies[3:]:
        copy.wait()
    em[...] = add(egv[...], eev[...]).astype(jnp.bfloat16)
    for p in range(ring):
        expand = dot(ecv[...], em[pl.ds(p * slab, slab), :], 1, 1)
        own = latent[:, p * latent_slab : (p + 1) * latent_slab]
        part[p] = jnp.concatenate([expand, own, rest], axis=1).astype(jnp.bfloat16)


def total(parts):
    whole = parts[0].astype(jnp.float32)
    for p in range(1, parts.shape[0]):
        whole = whole + parts[p].astype(jnp.float32)
    return whole


def sum_kernel(parts, out):
    piece = total(parts).astype(out.dtype)
    for p in range(out.shape[0]):
        out[p] = piece


def gram_kernel(slab, latent_slab, shard, pieces, out):
    shards, depth = pieces.shape[:2]
    half = RANK // 2
    gram = jnp.zeros((RANK, RANK), jnp.float32)
    every = jnp.zeros((RANK, LANES), jnp.float32)
    own = jnp.zeros((RANK, LANES), jnp.float32)
    for x in range(shards):
        piece = total(pieces.at[x])
        expand = piece[:, :slab]
        gram = gram + fine_dot(expand, expand, 1, 1)
        every = every + piece
        own = jnp.where(shard[0] == x, piece, own)
    lower = gram[half:, half:]
    corner = jnp.concatenate([lower[:, : half // 2], lower[:, half // 2 :]], axis=0)
    used = slab + latent_slab
    rest = jnp.zeros((RANK, LANES - used - half - half // 2), jnp.float32)
    mine = jnp.concatenate(
        [own[:, :slab], every[:, slab:used], gram[:, :half], corner, rest], axis=1
    )
    for p in range(out.shape[0]):
        out[p] = mine


def right_kernel(gathered, lm, em, gain, right, lb, eb):
    cores, line = gathered.shape[:2]
    ring = cores * line
    slab = em.shape[0] // ring
    used = slab + lm.shape[0] // ring
    half = RANK // 2
    places = [(p // line, p % line) for p in range(ring)]
    left = jnp.concatenate([gathered[c, y, :, slab:used] for c, y in places], axis=1)
    latent_gram = fine_dot(left, left, 1, 1)
    packed = total(gathered.at[0])
    for c in range(1, cores):
        packed = packed + total(gathered.at[c])
    first = packed[:, used : used + half]
    corner = packed[:, used + half : used + half + half // 2]
    corner = jnp.concatenate([corner[:half], corner[half:]], axis=1)
    second = jnp.concatenate([first[half:].T, corner], axis=0)
    expand_gram = jnp.concatenate([first, second], axis=1)
    latent_root, expand_root = inverse_roots([latent_gram, expand_gram])
    lb[...] = fine_dot(latent_root, left, 0, 0).astype(jnp.bfloat16)
    left = jnp.concatenate([gathered[c, y, :, :slab] for c, y in places], axis=1)
    eb[...] = fine_dot(expand_root, left, 0, 0).astype(jnp.bfloat16)
    tiles = [
        dot(lb[...], lm[...], 1, 0).astype(jnp.bfloat16),
        dot(eb[...], em[...], 1, 0).astype(jnp.bfloat16),
    ]
    p = 0
    for rows in range(0, RANK, half):
        for tile in tiles:
            for at in range(0, tile.shape[1], LANES):
                right[p] = tile[rows : rows + half, at : at + LANES]
                p += 1
    gains = [gain[:, at : at + LANES].astype(jnp.float32) for at in range(0, gain.shape[1], LANES)]
    gains.append(jnp.zeros((half - len(gains), LANES), jnp.float32))
    right[p] = jnp.concatenate(gains, axis=0).astype(jnp.bfloat16)
    for p in range(p + 1, ring):
        right[p] = jnp.zeros(right.shape[1:], right.dtype)


def halves(whole, is_gain):
    high = whole.astype(jnp.bfloat16).astype(jnp.float32)
    low = whole - high
    row = lax.broadcasted_iota(jnp.int32, whole.shape, 0)
    low = jnp.concatenate([low[:2], low[:2], low[4:]], axis=0)
    spare = jnp.logical_and(is_gain, jnp.logical_and(row >= 2, row < 4))
    return jnp.where(spare, low, high).astype(jnp.bfloat16)


def right_sum_kernel(gain_tile, ring, parts, out):
    piece = halves(total(parts), ring[0] == gain_tile)
    for p in range(out.shape[0]):
        out[p] = piece


def factor_kernel(gain_tile, latent_tiles, tiles, replicas, ring, shard, pieces, out):
    shards, depth = pieces.shape[:2]
    is_gain = ring[0] == gain_tile
    crossed = jnp.logical_and(ring[0] < gain_tile, lax.rem(ring[0], tiles) >= latent_tiles)
    whole = jnp.zeros(pieces.shape[2:], jnp.float32)
    for x in range(shards):
        piece = total(pieces.at[x])
        whole = whole + jnp.where(jnp.logical_or(crossed, shard[0] == x), piece, 0.0)
    whole = whole / replicas
    joined = jnp.concatenate([whole[:2] + whole[2:4], whole[2:]], axis=0)
    piece = halves(jnp.where(is_gain, joined, whole), is_gain)
    for p in range(out.shape[0]):
        out[p] = piece


def finish_kernel(shard, factors, lb, lg, le, lv, eb, eg, ee, ev, gv, *refs):
    ll, lmom, lf, el, emom, ef, gmom = refs[:7]
    llv, lmv, lfv, elv, emv, efv, gmv, sems = refs[7:]
    half = RANK // 2
    tiles = (lf.shape[1] + ef.shape[1]) // LANES
    copies = []

    def send(source, target):
        copies.append(pltpu.make_async_copy(source, target, sems.at[len(copies)]))
        copies[-1].start()

    first = 0
    for factor, out in ((lfv, lf), (efv, ef)):
        count = factor.shape[1] // LANES
        for t in range(count):
            for upper in range(2):
                factor[half * upper : half * (upper + 1), LANES * t : LANES * (t + 1)] = factors[
                    upper * tiles + first + t
                ]
        first += count
        send(factor, out)
    for basis, factor, grads, errors, moments, kept, leftover, fresh, momentum, cuts in (
        (eb, efv, eg, ee, ev, elv, el, emv, emom, EXPAND_CUTS),
        (lb, lfv, lg, le, lv, llv, ll, lmv, lmom, LATENT_CUTS),
    ):
        for low, high in zip(cuts, cuts[1:]):
            rows = pl.ds(low, high - low)
            approx = dot(basis[:, low:high], factor[...], 0, 0)
            whole = add(grads[0, rows, :], errors[0, rows, :])
            kept[rows, :] = (whole - approx).astype(jnp.bfloat16)
            send(kept.at[rows], leftover.at[0, rows])
            fresh[rows, :] = (BETA * moments[rows, :].astype(jnp.float32) + approx).astype(jnp.bfloat16)
            send(fresh.at[rows], momentum.at[rows])
    gain = factors[2 * tiles].astype(jnp.float32)
    gain = gain[:2] + gain[2:4]
    owned = gv.shape[1]
    mean = jnp.zeros((1, owned), jnp.float32)
    for x in range(2 * LANES // owned):
        at = x * owned
        own = gain[at // LANES : at // LANES + 1, at % LANES : at % LANES + owned]
        mean = jnp.where(shard[0] == x, own, mean)
    gmv[...] = BETA * gv[...] + mean
    send(gmv, gmom)
    for copy in copies:
        copy.wait()


def call(kernel, name, outs, args, scalars=0, fast=(), slow=(), scratch=()):
    args = list(args)
    specs = [pl.BlockSpec(memory_space=pltpu.SMEM)] * scalars
    for i in range(scalars, len(args)):
        space = pltpu.HBM if i in slow else pltpu.VMEM
        specs.append(pl.BlockSpec(memory_space=space))
        if i in slow or i in fast:
            args[i] = pltpu.with_memory_space_constraint(args[i], space)
    shapes = [
        pltpu.VMEM(shape, dtype) if near else jax.ShapeDtypeStruct(shape, dtype)
        for shape, dtype, near in outs
    ]
    return pl.pallas_call(
        kernel,
        out_shape=shapes,
        in_specs=specs,
        out_specs=[pl.BlockSpec(memory_space=pltpu.VMEM if near else pl.ANY) for *_, near in outs],
        scratch_shapes=scratch,
        compiler_params=pltpu.CompilerParams(vmem_limit_bytes=16 << 20),
        name=name,
    )(*args)


def exchange(array, axes):
    return lax.all_to_all(array, axes, 0, 0)


def local(
    latent_grads,
    latent_errors,
    latent_moments,
    latent_coeffs,
    expand_grads,
    expand_errors,
    expand_moments,
    expand_coeffs,
    gain_grads,
    gain_moments,
):
    ring = lax.axis_size(RING)
    depth = lax.axis_size("z")
    shards = lax.axis_size("x")
    cross = depth * shards
    shard = lax.axis_index("x").astype(jnp.int32).reshape(1)
    place = lax.axis_index(RING).astype(jnp.int32).reshape(1)
    latent_rows, latent_cols = latent_grads.shape[1:]
    expand_rows, expand_cols = expand_grads.shape[1:]
    slab = expand_rows // ring
    latent_slab = latent_rows // ring
    latent_tiles = latent_cols // LANES
    tiles = latent_tiles + expand_cols // LANES
    half = RANK // 2
    bf16, f32 = jnp.bfloat16, jnp.float32

    latent_shape, expand_shape = (latent_rows, latent_cols), (expand_rows, expand_cols)
    owned = (1, gain_moments.shape[0])
    part, latent_merged, expand_merged, own_gain, gain_before = call(
        left_kernel,
        "left",
        (
            ((ring, RANK, LANES), bf16, True),
            (latent_shape, bf16, True),
            (expand_shape, bf16, True),
            (gain_grads.shape, bf16, True),
            (owned, f32, True),
        ),
        (
            latent_grads,
            latent_errors,
            latent_coeffs.T,
            expand_grads,
            expand_errors,
            expand_coeffs.T,
            gain_grads,
            gain_moments.reshape(owned),
        ),
        slow=range(8),
        scratch=(
            pltpu.VMEM(latent_shape, bf16),
            pltpu.VMEM(latent_shape, bf16),
            pltpu.VMEM((RANK, latent_cols), bf16),
            pltpu.VMEM(expand_shape, bf16),
            pltpu.VMEM(expand_shape, bf16),
            pltpu.VMEM((RANK, expand_cols), bf16),
            pltpu.SemaphoreType.DMA((8,)),
        ),
    )
    part, shard, place = lax.optimization_barrier((part, shard, place))
    part = exchange(part, RING)
    (piece,) = call(sum_kernel, "left_sum", (((cross, RANK, LANES), bf16, True),), (part,), 0, (0,))
    pieces = exchange(piece, CROSS).reshape(shards, depth, RANK, LANES)
    (mine,) = call(
        functools.partial(gram_kernel, slab, latent_slab),
        "gram",
        (((lax.axis_size("y"), RANK, LANES), f32, True),),
        (shard, pieces),
        1,
        (1,),
    )
    gathered = lax.all_gather(exchange(mine, "y"), "core")
    right, latent_basis, expand_basis = call(
        right_kernel,
        "right",
        (
            ((ring, half, LANES), bf16, True),
            ((RANK, latent_rows), bf16, True),
            ((RANK, expand_rows), bf16, True),
        ),
        (gathered, latent_merged, expand_merged, own_gain),
        0,
        range(4),
    )
    right = exchange(right, RING)
    (piece,) = call(
        functools.partial(right_sum_kernel, 2 * tiles),
        "right_sum",
        (((cross, half, LANES), bf16, True),),
        (place, right),
        1,
        (1,),
    )
    pieces = exchange(piece, CROSS).reshape(shards, depth, half, LANES)
    (mine,) = call(
        functools.partial(factor_kernel, 2 * tiles, latent_tiles, tiles, ring * depth),
        "factor",
        (((ring, half, LANES), bf16, True),),
        (place, shard, pieces),
        2,
        (2,),
    )
    factors = exchange(mine, RING)
    latent_factor, expand_factor = (RANK, latent_cols), (RANK, expand_cols)
    outs = call(
        finish_kernel,
        "finish",
        (
            ((1, *latent_shape), bf16, False),
            (latent_shape, bf16, False),
            (latent_factor, bf16, False),
            ((1, *expand_shape), bf16, False),
            (expand_shape, bf16, False),
            (expand_factor, bf16, False),
            (owned, f32, False),
        ),
        (
            shard,
            factors,
            latent_basis,
            latent_grads,
            latent_errors,
            latent_moments,
            expand_basis,
            expand_grads,
            expand_errors,
            expand_moments,
            gain_before,
        ),
        scalars=1,
        fast=range(1, 11),
        scratch=(
            pltpu.VMEM(latent_shape, bf16),
            pltpu.VMEM(latent_shape, bf16),
            pltpu.VMEM(latent_factor, bf16),
            pltpu.VMEM(expand_shape, bf16),
            pltpu.VMEM(expand_shape, bf16),
            pltpu.VMEM(expand_factor, bf16),
            pltpu.VMEM(owned, f32),
            pltpu.SemaphoreType.DMA((3 + 2 * (len(EXPAND_CUTS) + len(LATENT_CUTS) - 2),)),
        ),
    )
    return (*outs[:2], outs[2].T, *outs[3:5], outs[5].T, outs[6].reshape(-1))


def solution(mesh):
    grid = Mesh(mesh.devices.reshape(8, 8, 2, 4), ("z", "y", "core", "x"))
    return jax.shard_map(
        local,
        mesh=grid,
        in_specs=(
            P(DP, None, "x"),
            P(DP, None, "x"),
            P(None, "x"),
            P("x", None),
            P(DP, "x", None),
            P(DP, "x", None),
            P("x", None),
            P(),
            P(DP, None),
            P("x"),
        ),
        out_specs=(
            P(DP, None, "x"),
            P(None, "x"),
            P("x", None),
            P(DP, "x", None),
            P("x", None),
            P(),
            P("x"),
        ),
        check_vma=False,
    )
```

```python
import functools

import jax
import jax.numpy as jnp
from jax import lax
from jax.experimental import pallas as pl
from jax.experimental.pallas import tpu as pltpu
from jax.sharding import Mesh, PartitionSpec as P

NS_ITERS = 6
BETA = 0.9
EPSILON = 1e-06
RANK = 32
LANES = 128
EXPAND_CUTS = (0, 128, 512, 896, 1280)
LATENT_CUTS = (0, 288)
LEFT_OWNERS = ("core", "y")
LEFT_CROSS = ("x", "z")
RIGHT_OWNERS = ("core", "z")
RIGHT_CROSS = ("x", "y")
DP = ("z", "y", "core")


def dot(left, right, left_dim, right_dim):
    dims = (((left_dim,), (right_dim,)), ((), ()))
    return lax.dot_general(left, right, dims, preferred_element_type=jnp.float32)


def split(whole):
    high = whole.astype(jnp.bfloat16)
    return high, (whole - high.astype(jnp.float32)).astype(jnp.bfloat16)


def fine_dot(left, right, left_dim, right_dim):
    (lh, ll), (rh, rl) = split(left), split(right)
    small = dot(lh, rl, left_dim, right_dim) + dot(ll, rh, left_dim, right_dim)
    return dot(lh, rh, left_dim, right_dim) + small


def inverse_roots(grams):
    row = lax.broadcasted_iota(jnp.int32, (RANK, RANK), 0)
    column = lax.broadcasted_iota(jnp.int32, (RANK, RANK), 1)
    identity = jnp.where(row == column, jnp.float32(1), jnp.float32(0))
    traces = [jnp.sum(g * identity, keepdims=True) + EPSILON for g in grams]
    lefts = [g / t for g, t in zip(grams, traces)]
    middles = [1.5 * identity - 0.5 * y for y in lefts]
    rights = middles
    for repeat_index in range(1, NS_ITERS):
        lefts = [fine_dot(y, m, 1, 0) for y, m in zip(lefts, middles)]
        middles = [
            1.5 * identity - 0.5 * fine_dot(z, y, 1, 0) for z, y in zip(rights, lefts)
        ]
        rights = [fine_dot(m, z, 1, 0) for m, z in zip(middles, rights)]
    return [z / jnp.sqrt(t) for z, t in zip(rights, traces)]


def add(left, right):
    return left.astype(jnp.float32) + right.astype(jnp.float32)


def left_kernel(lg, le, lc, eg, ee, ec, gg, gm, part, lm, em, ggv, gmv, lgv, lev, lcv, egv, eev, ecv, sems):
    ring = part.shape[0]
    slab = em.shape[0] // ring
    latent_slab = lm.shape[0] // ring
    copies = []

    def fetch(source, target):
        copies.append(pltpu.make_async_copy(source, target, sems.at[len(copies)]))
        copies[-1].start()

    fetch(lc, lcv)
    fetch(lg.at[0], lgv)
    fetch(le.at[0], lev)
    fetch(ec, ecv)
    fetch(eg.at[0], egv)
    fetch(ee.at[0], eev)
    fetch(gg, ggv)
    fetch(gm, gmv)
    for c in range(3):
        copies[c].wait()
    lm[...] = add(lgv[...], lev[...]).astype(jnp.bfloat16)
    latent = dot(lcv[...], lm[...], 1, 1)
    rest = jnp.zeros((RANK, LANES - slab - latent_slab), jnp.float32)
    for copy in copies[3:]:
        copy.wait()
    em[...] = add(egv[...], eev[...]).astype(jnp.bfloat16)
    for p in range(ring):
        expand = dot(ecv[...], em[pl.ds(p * slab, slab), :], 1, 1)
        own = latent[:, p * latent_slab : (p + 1) * latent_slab]
        part[p] = jnp.concatenate([expand, own, rest], axis=1).astype(jnp.bfloat16)


def total(parts):
    whole = parts[0].astype(jnp.float32)
    for p in range(1, parts.shape[0]):
        whole = whole + parts[p].astype(jnp.float32)
    return whole


def sum_kernel(parts, out):
    piece = total(parts).astype(out.dtype)
    for p in range(out.shape[0]):
        out[p] = piece


def gram_kernel(slab, latent_slab, shard, pieces, out):
    shards, depth = pieces.shape[:2]
    half = RANK // 2
    gram = jnp.zeros((RANK, RANK), jnp.float32)
    every = jnp.zeros((RANK, LANES), jnp.float32)
    own = jnp.zeros((RANK, LANES), jnp.float32)
    for x in range(shards):
        piece = total(pieces.at[x])
        expand = piece[:, :slab]
        gram = gram + fine_dot(expand, expand, 1, 1)
        every = every + piece
        own = jnp.where(shard[0] == x, piece, own)
    lower = gram[half:, half:]
    corner = jnp.concatenate([lower[:, : half // 2], lower[:, half // 2 :]], axis=0)
    used = slab + latent_slab
    rest = jnp.zeros((RANK, LANES - used - half - half // 2), jnp.float32)
    mine = jnp.concatenate(
        [own[:, :slab], every[:, slab:used], gram[:, :half], corner, rest], axis=1
    )
    for p in range(out.shape[0]):
        out[p] = mine


def right_kernel(gathered, lm, em, gain, right, lb, eb):
    cores, line = gathered.shape[:2]
    ring = cores * line
    slab = em.shape[0] // ring
    used = slab + lm.shape[0] // ring
    half = RANK // 2
    places = [(p // line, p % line) for p in range(ring)]
    left = jnp.concatenate([gathered[c, y, :, slab:used] for c, y in places], axis=1)
    latent_gram = fine_dot(left, left, 1, 1)
    packed = total(gathered.at[0])
    for c in range(1, cores):
        packed = packed + total(gathered.at[c])
    first = packed[:, used : used + half]
    corner = packed[:, used + half : used + half + half // 2]
    corner = jnp.concatenate([corner[:half], corner[half:]], axis=1)
    second = jnp.concatenate([first[half:].T, corner], axis=0)
    expand_gram = jnp.concatenate([first, second], axis=1)
    latent_root, expand_root = inverse_roots([latent_gram, expand_gram])
    lb[...] = fine_dot(latent_root, left, 0, 0).astype(jnp.bfloat16)
    left = jnp.concatenate([gathered[c, y, :, :slab] for c, y in places], axis=1)
    eb[...] = fine_dot(expand_root, left, 0, 0).astype(jnp.bfloat16)
    tiles = [
        dot(lb[...], lm[...], 1, 0).astype(jnp.bfloat16),
        dot(eb[...], em[...], 1, 0).astype(jnp.bfloat16),
    ]
    p = 0
    for rows in range(0, RANK, half):
        for tile in tiles:
            for at in range(0, tile.shape[1], LANES):
                right[p] = tile[rows : rows + half, at : at + LANES]
                p += 1
    gains = [gain[:, at : at + LANES].astype(jnp.float32) for at in range(0, gain.shape[1], LANES)]
    gains.append(jnp.zeros((half - len(gains), LANES), jnp.float32))
    right[p] = jnp.concatenate(gains, axis=0).astype(jnp.bfloat16)
    for p in range(p + 1, ring):
        right[p] = jnp.zeros(right.shape[1:], right.dtype)


def halves(whole, is_gain):
    high = whole.astype(jnp.bfloat16).astype(jnp.float32)
    low = whole - high
    row = lax.broadcasted_iota(jnp.int32, whole.shape, 0)
    low = jnp.concatenate([low[:2], low[:2], low[4:]], axis=0)
    spare = jnp.logical_and(is_gain, jnp.logical_and(row >= 2, row < 4))
    return jnp.where(spare, low, high).astype(jnp.bfloat16)


def right_sum_kernel(gain_tile, ring, parts, out):
    piece = halves(total(parts), ring[0] == gain_tile)
    for p in range(out.shape[0]):
        out[p] = piece


def factor_kernel(gain_tile, latent_tiles, tiles, replicas, ring, shard, pieces, out):
    shards, depth = pieces.shape[:2]
    is_gain = ring[0] == gain_tile
    crossed = jnp.logical_and(ring[0] < gain_tile, lax.rem(ring[0], tiles) >= latent_tiles)
    whole = jnp.zeros(pieces.shape[2:], jnp.float32)
    for x in range(shards):
        piece = total(pieces.at[x])
        whole = whole + jnp.where(jnp.logical_or(crossed, shard[0] == x), piece, 0.0)
    whole = whole / replicas
    joined = jnp.concatenate([whole[:2] + whole[2:4], whole[2:]], axis=0)
    piece = halves(jnp.where(is_gain, joined, whole), is_gain)
    for p in range(out.shape[0]):
        out[p] = piece


def finish_kernel(shard, factors, lb, lg, le, lv, eb, eg, ee, ev, gv, *refs):
    ll, lmom, lf, el, emom, ef, gmom = refs[:7]
    llv, lmv, lfv, elv, emv, efv, gmv, sems = refs[7:]
    half = RANK // 2
    tiles = (lf.shape[1] + ef.shape[1]) // LANES
    copies = []

    def send(source, target):
        copies.append(pltpu.make_async_copy(source, target, sems.at[len(copies)]))
        copies[-1].start()

    first = 0
    for factor, out in ((lfv, lf), (efv, ef)):
        count = factor.shape[1] // LANES
        for t in range(count):
            for upper in range(2):
                factor[half * upper : half * (upper + 1), LANES * t : LANES * (t + 1)] = factors[
                    upper * tiles + first + t
                ]
        first += count
        send(factor, out)
    for basis, factor, grads, errors, moments, kept, leftover, fresh, momentum, cuts in (
        (eb, efv, eg, ee, ev, elv, el, emv, emom, EXPAND_CUTS),
        (lb, lfv, lg, le, lv, llv, ll, lmv, lmom, LATENT_CUTS),
    ):
        for low, high in zip(cuts, cuts[1:]):
            rows = pl.ds(low, high - low)
            approx = dot(basis[:, low:high], factor[...], 0, 0)
            whole = add(grads[0, rows, :], errors[0, rows, :])
            kept[rows, :] = (whole - approx).astype(jnp.bfloat16)
            send(kept.at[rows], leftover.at[0, rows])
            fresh[rows, :] = (BETA * moments[rows, :].astype(jnp.float32) + approx).astype(jnp.bfloat16)
            send(fresh.at[rows], momentum.at[rows])
    gain = factors[2 * tiles].astype(jnp.float32)
    gain = gain[:2] + gain[2:4]
    owned = gv.shape[1]
    mean = jnp.zeros((1, owned), jnp.float32)
    for x in range(2 * LANES // owned):
        at = x * owned
        own = gain[at // LANES : at // LANES + 1, at % LANES : at % LANES + owned]
        mean = jnp.where(shard[0] == x, own, mean)
    gmv[...] = BETA * gv[...] + mean
    send(gmv, gmom)
    for copy in copies:
        copy.wait()


def call(kernel, name, outs, args, scalars=0, fast=(), slow=(), scratch=()):
    args = list(args)
    specs = [pl.BlockSpec(memory_space=pltpu.SMEM)] * scalars
    for i in range(scalars, len(args)):
        space = pltpu.HBM if i in slow else pltpu.VMEM
        specs.append(pl.BlockSpec(memory_space=space))
        if i in slow or i in fast:
            args[i] = pltpu.with_memory_space_constraint(args[i], space)
    shapes = [
        pltpu.VMEM(shape, dtype) if near else jax.ShapeDtypeStruct(shape, dtype)
        for shape, dtype, near in outs
    ]
    return pl.pallas_call(
        kernel,
        out_shape=shapes,
        in_specs=specs,
        out_specs=[pl.BlockSpec(memory_space=pltpu.VMEM if near else pl.ANY) for *_, near in outs],
        scratch_shapes=scratch,
        compiler_params=pltpu.CompilerParams(vmem_limit_bytes=16 << 20),
        name=name,
    )(*args)


def exchange(array, axes):
    return lax.all_to_all(array, axes, 0, 0)


def local(
    latent_grads,
    latent_errors,
    latent_moments,
    latent_coeffs,
    expand_grads,
    expand_errors,
    expand_moments,
    expand_coeffs,
    gain_grads,
    gain_moments,
):
    ring = lax.axis_size(LEFT_OWNERS)
    depth = lax.axis_size("z")
    shards = lax.axis_size("x")
    cross = depth * shards
    shard = lax.axis_index("x").astype(jnp.int32).reshape(1)
    place = lax.axis_index(RIGHT_OWNERS).astype(jnp.int32).reshape(1)
    latent_rows, latent_cols = latent_grads.shape[1:]
    expand_rows, expand_cols = expand_grads.shape[1:]
    slab = expand_rows // ring
    latent_slab = latent_rows // ring
    latent_tiles = latent_cols // LANES
    tiles = latent_tiles + expand_cols // LANES
    half = RANK // 2
    bf16, f32 = jnp.bfloat16, jnp.float32

    latent_shape, expand_shape = (latent_rows, latent_cols), (expand_rows, expand_cols)
    owned = (1, gain_moments.shape[0])
    part, latent_merged, expand_merged, own_gain, gain_before = call(
        left_kernel,
        "left",
        (
            ((ring, RANK, LANES), bf16, True),
            (latent_shape, bf16, True),
            (expand_shape, bf16, True),
            (gain_grads.shape, bf16, True),
            (owned, f32, True),
        ),
        (
            latent_grads,
            latent_errors,
            latent_coeffs.T,
            expand_grads,
            expand_errors,
            expand_coeffs.T,
            gain_grads,
            gain_moments.reshape(owned),
        ),
        slow=range(8),
        scratch=(
            pltpu.VMEM(latent_shape, bf16),
            pltpu.VMEM(latent_shape, bf16),
            pltpu.VMEM((RANK, latent_cols), bf16),
            pltpu.VMEM(expand_shape, bf16),
            pltpu.VMEM(expand_shape, bf16),
            pltpu.VMEM((RANK, expand_cols), bf16),
            pltpu.SemaphoreType.DMA((8,)),
        ),
    )
    part, shard, place = lax.optimization_barrier((part, shard, place))
    part = exchange(part, LEFT_OWNERS)
    (piece,) = call(sum_kernel, "left_sum", (((cross, RANK, LANES), bf16, True),), (part,), 0, (0,))
    pieces = exchange(piece, LEFT_CROSS).reshape(shards, depth, RANK, LANES)
    (mine,) = call(
        functools.partial(gram_kernel, slab, latent_slab),
        "gram",
        (((lax.axis_size("y"), RANK, LANES), f32, True),),
        (shard, pieces),
        1,
        (1,),
    )
    gathered = lax.all_gather(exchange(mine, "y"), "core")
    right, latent_basis, expand_basis = call(
        right_kernel,
        "right",
        (
            ((ring, half, LANES), bf16, True),
            ((RANK, latent_rows), bf16, True),
            ((RANK, expand_rows), bf16, True),
        ),
        (gathered, latent_merged, expand_merged, own_gain),
        0,
        range(4),
    )
    right = exchange(right, RIGHT_OWNERS)
    (piece,) = call(
        functools.partial(right_sum_kernel, 2 * tiles),
        "right_sum",
        (((cross, half, LANES), bf16, True),),
        (place, right),
        1,
        (1,),
    )
    pieces = exchange(piece, RIGHT_CROSS).reshape(shards, depth, half, LANES)
    (mine,) = call(
        functools.partial(factor_kernel, 2 * tiles, latent_tiles, tiles, ring * depth),
        "factor",
        (((ring, half, LANES), bf16, True),),
        (place, shard, pieces),
        2,
        (2,),
    )
    factors = exchange(mine, RIGHT_OWNERS)
    latent_factor, expand_factor = (RANK, latent_cols), (RANK, expand_cols)
    outs = call(
        finish_kernel,
        "finish",
        (
            ((1, *latent_shape), bf16, False),
            (latent_shape, bf16, False),
            (latent_factor, bf16, False),
            ((1, *expand_shape), bf16, False),
            (expand_shape, bf16, False),
            (expand_factor, bf16, False),
            (owned, f32, False),
        ),
        (
            shard,
            factors,
            latent_basis,
            latent_grads,
            latent_errors,
            latent_moments,
            expand_basis,
            expand_grads,
            expand_errors,
            expand_moments,
            gain_before,
        ),
        scalars=1,
        fast=range(1, 11),
        scratch=(
            pltpu.VMEM(latent_shape, bf16),
            pltpu.VMEM(latent_shape, bf16),
            pltpu.VMEM(latent_factor, bf16),
            pltpu.VMEM(expand_shape, bf16),
            pltpu.VMEM(expand_shape, bf16),
            pltpu.VMEM(expand_factor, bf16),
            pltpu.VMEM(owned, f32),
            pltpu.SemaphoreType.DMA((3 + 2 * (len(EXPAND_CUTS) + len(LATENT_CUTS) - 2),)),
        ),
    )
    return (*outs[:2], outs[2].T, *outs[3:5], outs[5].T, outs[6].reshape(-1))


def solution(mesh):
    grid = Mesh(mesh.devices.reshape(8, 8, 2, 4), ("z", "y", "core", "x"))
    return jax.shard_map(
        local,
        mesh=grid,
        in_specs=(
            P(DP, None, "x"),
            P(DP, None, "x"),
            P(None, "x"),
            P("x", None),
            P(DP, "x", None),
            P(DP, "x", None),
            P("x", None),
            P(),
            P(DP, None),
            P("x"),
        ),
        out_specs=(
            P(DP, None, "x"),
            P(None, "x"),
            P("x", None),
            P(DP, "x", None),
            P("x", None),
            P(),
            P("x"),
        ),
        check_vma=False,
    )
```

```python
import functools

import jax
import jax.numpy as jnp
from jax import lax
from jax.experimental import pallas as pl
from jax.experimental.pallas import tpu as pltpu
from jax.sharding import Mesh, PartitionSpec as P

NS_ITERS = 6
BETA = 0.9
EPSILON = 1e-06
RANK = 32
LANES = 128
EXPAND_CUTS = (0, 128, 512, 896, 1280)
LATENT_CUTS = (0, 288)
LEFT_OWNERS = ("core", "y")
LEFT_CROSS = ("x", "z")
RIGHT_OWNERS = ("core", "z")
RIGHT_CROSS = ("x", "y")
DP = ("z", "y", "core")


def dot(left, right, left_dim, right_dim):
    dims = (((left_dim,), (right_dim,)), ((), ()))
    return lax.dot_general(left, right, dims, preferred_element_type=jnp.float32)


def split(whole):
    high = whole.astype(jnp.bfloat16)
    return high, (whole - high.astype(jnp.float32)).astype(jnp.bfloat16)


def fine_dot(left, right, left_dim, right_dim):
    (lh, ll), (rh, rl) = split(left), split(right)
    small = dot(lh, rl, left_dim, right_dim) + dot(ll, rh, left_dim, right_dim)
    return dot(lh, rh, left_dim, right_dim) + small


def inverse_roots(grams):
    row = lax.broadcasted_iota(jnp.int32, (RANK, RANK), 0)
    column = lax.broadcasted_iota(jnp.int32, (RANK, RANK), 1)
    identity = jnp.where(row == column, jnp.float32(1), jnp.float32(0))
    traces = [jnp.sum(g * identity, keepdims=True) + EPSILON for g in grams]
    lefts = [g / t for g, t in zip(grams, traces)]
    middles = [1.5 * identity - 0.5 * y for y in lefts]
    rights = middles
    for repeat_index in range(1, NS_ITERS):
        lefts = [fine_dot(y, m, 1, 0) for y, m in zip(lefts, middles)]
        middles = [
            1.5 * identity - 0.5 * fine_dot(z, y, 1, 0) for z, y in zip(rights, lefts)
        ]
        rights = [fine_dot(m, z, 1, 0) for m, z in zip(middles, rights)]
    return [z / jnp.sqrt(t) for z, t in zip(rights, traces)]


def add(left, right):
    return left.astype(jnp.float32) + right.astype(jnp.float32)


def left_kernel(lg, le, lc, eg, ee, ec, gg, gm, part, lm, em, ggv, gmv, lgv, lev, lcv, egv, eev, ecv, sems):
    ring = part.shape[0]
    slab = em.shape[0] // ring
    latent_slab = lm.shape[0] // ring
    copies = []

    def fetch(source, target):
        copies.append(pltpu.make_async_copy(source, target, sems.at[len(copies)]))
        copies[-1].start()

    fetch(lc, lcv)
    fetch(lg.at[0], lgv)
    fetch(le.at[0], lev)
    fetch(ec, ecv)
    fetch(eg.at[0], egv)
    fetch(ee.at[0], eev)
    fetch(gg, ggv)
    fetch(gm, gmv)
    for c in range(3):
        copies[c].wait()
    lm[...] = add(lgv[...], lev[...]).astype(jnp.bfloat16)
    latent = dot(lcv[...], lm[...], 1, 1)
    rest = jnp.zeros((RANK, LANES - slab - latent_slab), jnp.float32)
    for copy in copies[3:6]:
        copy.wait()
    em[...] = add(egv[...], eev[...]).astype(jnp.bfloat16)
    for p in range(ring):
        expand = dot(ecv[...], em[pl.ds(p * slab, slab), :], 1, 1)
        own = latent[:, p * latent_slab : (p + 1) * latent_slab]
        part[p] = jnp.concatenate([expand, own, rest], axis=1).astype(jnp.bfloat16)
    for copy in copies[6:]:
        copy.wait()


def total(parts):
    whole = parts[0].astype(jnp.float32)
    for p in range(1, parts.shape[0]):
        whole = whole + parts[p].astype(jnp.float32)
    return whole


def sum_kernel(parts, out):
    piece = total(parts).astype(out.dtype)
    for p in range(out.shape[0]):
        out[p] = piece


def gram_kernel(slab, latent_slab, shard, pieces, out):
    shards, depth = pieces.shape[:2]
    half = RANK // 2
    gram = jnp.zeros((RANK, RANK), jnp.float32)
    every = jnp.zeros((RANK, LANES), jnp.float32)
    own = jnp.zeros((RANK, LANES), jnp.float32)
    for x in range(shards):
        piece = total(pieces.at[x])
        expand = piece[:, :slab]
        gram = gram + fine_dot(expand, expand, 1, 1)
        every = every + piece
        own = jnp.where(shard[0] == x, piece, own)
    lower = gram[half:, half:]
    corner = jnp.concatenate([lower[:, : half // 2], lower[:, half // 2 :]], axis=0)
    used = slab + latent_slab
    rest = jnp.zeros((RANK, LANES - used - half - half // 2), jnp.float32)
    mine = jnp.concatenate(
        [own[:, :slab], every[:, slab:used], gram[:, :half], corner, rest], axis=1
    )
    for p in range(out.shape[0]):
        out[p] = mine


def right_kernel(gathered, lm, em, gain, right, lb, eb):
    cores, line = gathered.shape[:2]
    ring = cores * line
    slab = em.shape[0] // ring
    used = slab + lm.shape[0] // ring
    half = RANK // 2
    places = [(p // line, p % line) for p in range(ring)]
    left = jnp.concatenate([gathered[c, y, :, slab:used] for c, y in places], axis=1)
    latent_gram = fine_dot(left, left, 1, 1)
    packed = total(gathered.at[0])
    for c in range(1, cores):
        packed = packed + total(gathered.at[c])
    first = packed[:, used : used + half]
    corner = packed[:, used + half : used + half + half // 2]
    corner = jnp.concatenate([corner[:half], corner[half:]], axis=1)
    second = jnp.concatenate([first[half:].T, corner], axis=0)
    expand_gram = jnp.concatenate([first, second], axis=1)
    latent_root, expand_root = inverse_roots([latent_gram, expand_gram])
    lb[...] = fine_dot(latent_root, left, 0, 0).astype(jnp.bfloat16)
    left = jnp.concatenate([gathered[c, y, :, :slab] for c, y in places], axis=1)
    eb[...] = fine_dot(expand_root, left, 0, 0).astype(jnp.bfloat16)
    tiles = [
        dot(lb[...], lm[...], 1, 0).astype(jnp.bfloat16),
        dot(eb[...], em[...], 1, 0).astype(jnp.bfloat16),
    ]
    p = 0
    for rows in range(0, RANK, half):
        for tile in tiles:
            for at in range(0, tile.shape[1], LANES):
                right[p] = tile[rows : rows + half, at : at + LANES]
                p += 1
    gains = [gain[:, at : at + LANES].astype(jnp.float32) for at in range(0, gain.shape[1], LANES)]
    gains.append(jnp.zeros((half - len(gains), LANES), jnp.float32))
    right[p] = jnp.concatenate(gains, axis=0).astype(jnp.bfloat16)
    for p in range(p + 1, ring):
        right[p] = jnp.zeros(right.shape[1:], right.dtype)


def halves(whole, is_gain):
    high = whole.astype(jnp.bfloat16).astype(jnp.float32)
    low = whole - high
    row = lax.broadcasted_iota(jnp.int32, whole.shape, 0)
    low = jnp.concatenate([low[:2], low[:2], low[4:]], axis=0)
    spare = jnp.logical_and(is_gain, jnp.logical_and(row >= 2, row < 4))
    return jnp.where(spare, low, high).astype(jnp.bfloat16)


def right_sum_kernel(gain_tile, ring, parts, out):
    piece = halves(total(parts), ring[0] == gain_tile)
    for p in range(out.shape[0]):
        out[p] = piece


def factor_kernel(gain_tile, latent_tiles, tiles, replicas, ring, shard, pieces, out):
    shards, depth = pieces.shape[:2]
    is_gain = ring[0] == gain_tile
    crossed = jnp.logical_and(ring[0] < gain_tile, lax.rem(ring[0], tiles) >= latent_tiles)
    whole = jnp.zeros(pieces.shape[2:], jnp.float32)
    for x in range(shards):
        piece = total(pieces.at[x])
        whole = whole + jnp.where(jnp.logical_or(crossed, shard[0] == x), piece, 0.0)
    whole = whole / replicas
    joined = jnp.concatenate([whole[:2] + whole[2:4], whole[2:]], axis=0)
    piece = halves(jnp.where(is_gain, joined, whole), is_gain)
    for p in range(out.shape[0]):
        out[p] = piece


def finish_kernel(shard, factors, lb, lg, le, lv, eb, eg, ee, ev, gv, *refs):
    ll, lmom, lf, el, emom, ef, gmom = refs[:7]
    llv, lmv, lfv, elv, emv, efv, gmv, sems = refs[7:]
    half = RANK // 2
    tiles = (lf.shape[1] + ef.shape[1]) // LANES
    copies = []

    def send(source, target):
        copies.append(pltpu.make_async_copy(source, target, sems.at[len(copies)]))
        copies[-1].start()

    first = 0
    for factor, out in ((lfv, lf), (efv, ef)):
        count = factor.shape[1] // LANES
        for t in range(count):
            for upper in range(2):
                factor[half * upper : half * (upper + 1), LANES * t : LANES * (t + 1)] = factors[
                    upper * tiles + first + t
                ]
        first += count
        send(factor, out)
    for basis, factor, grads, errors, moments, kept, leftover, fresh, momentum, cuts in (
        (eb, efv, eg, ee, ev, elv, el, emv, emom, EXPAND_CUTS),
        (lb, lfv, lg, le, lv, llv, ll, lmv, lmom, LATENT_CUTS),
    ):
        for low, high in zip(cuts, cuts[1:]):
            rows = pl.ds(low, high - low)
            approx = dot(basis[:, low:high], factor[...], 0, 0)
            whole = add(grads[0, rows, :], errors[0, rows, :])
            kept[rows, :] = (whole - approx).astype(jnp.bfloat16)
            send(kept.at[rows], leftover.at[0, rows])
            fresh[rows, :] = (BETA * moments[rows, :].astype(jnp.float32) + approx).astype(jnp.bfloat16)
            send(fresh.at[rows], momentum.at[rows])
    gain = factors[2 * tiles].astype(jnp.float32)
    gain = gain[:2] + gain[2:4]
    owned = gv.shape[1]
    mean = jnp.zeros((1, owned), jnp.float32)
    for x in range(2 * LANES // owned):
        at = x * owned
        own = gain[at // LANES : at // LANES + 1, at % LANES : at % LANES + owned]
        mean = jnp.where(shard[0] == x, own, mean)
    gmv[...] = BETA * gv[...] + mean
    send(gmv, gmom)
    for copy in copies:
        copy.wait()


def call(kernel, name, outs, args, scalars=0, fast=(), slow=(), scratch=()):
    args = list(args)
    specs = [pl.BlockSpec(memory_space=pltpu.SMEM)] * scalars
    for i in range(scalars, len(args)):
        space = pltpu.HBM if i in slow else pltpu.VMEM
        specs.append(pl.BlockSpec(memory_space=space))
        if i in slow or i in fast:
            args[i] = pltpu.with_memory_space_constraint(args[i], space)
    shapes = [
        pltpu.VMEM(shape, dtype) if near else jax.ShapeDtypeStruct(shape, dtype)
        for shape, dtype, near in outs
    ]
    return pl.pallas_call(
        kernel,
        out_shape=shapes,
        in_specs=specs,
        out_specs=[pl.BlockSpec(memory_space=pltpu.VMEM if near else pl.ANY) for *_, near in outs],
        scratch_shapes=scratch,
        compiler_params=pltpu.CompilerParams(vmem_limit_bytes=16 << 20),
        name=name,
    )(*args)


def exchange(array, axes):
    return lax.all_to_all(array, axes, 0, 0)


def local(
    latent_grads,
    latent_errors,
    latent_moments,
    latent_coeffs,
    expand_grads,
    expand_errors,
    expand_moments,
    expand_coeffs,
    gain_grads,
    gain_moments,
):
    ring = lax.axis_size(LEFT_OWNERS)
    depth = lax.axis_size("z")
    shards = lax.axis_size("x")
    cross = depth * shards
    shard = lax.axis_index("x").astype(jnp.int32).reshape(1)
    place = lax.axis_index(RIGHT_OWNERS).astype(jnp.int32).reshape(1)
    latent_rows, latent_cols = latent_grads.shape[1:]
    expand_rows, expand_cols = expand_grads.shape[1:]
    slab = expand_rows // ring
    latent_slab = latent_rows // ring
    latent_tiles = latent_cols // LANES
    tiles = latent_tiles + expand_cols // LANES
    half = RANK // 2
    bf16, f32 = jnp.bfloat16, jnp.float32

    latent_shape, expand_shape = (latent_rows, latent_cols), (expand_rows, expand_cols)
    owned = (1, gain_moments.shape[0])
    part, latent_merged, expand_merged, own_gain, gain_before = call(
        left_kernel,
        "left",
        (
            ((ring, RANK, LANES), bf16, True),
            (latent_shape, bf16, True),
            (expand_shape, bf16, True),
            (gain_grads.shape, bf16, True),
            (owned, f32, True),
        ),
        (
            latent_grads,
            latent_errors,
            latent_coeffs.T,
            expand_grads,
            expand_errors,
            expand_coeffs.T,
            gain_grads,
            gain_moments.reshape(owned),
        ),
        slow=range(8),
        scratch=(
            pltpu.VMEM(latent_shape, bf16),
            pltpu.VMEM(latent_shape, bf16),
            pltpu.VMEM((RANK, latent_cols), bf16),
            pltpu.VMEM(expand_shape, bf16),
            pltpu.VMEM(expand_shape, bf16),
            pltpu.VMEM((RANK, expand_cols), bf16),
            pltpu.SemaphoreType.DMA((8,)),
        ),
    )
    part, shard, place = lax.optimization_barrier((part, shard, place))
    part = exchange(part, LEFT_OWNERS)
    (piece,) = call(sum_kernel, "left_sum", (((cross, RANK, LANES), bf16, True),), (part,), 0, (0,))
    pieces = exchange(piece, LEFT_CROSS).reshape(shards, depth, RANK, LANES)
    (mine,) = call(
        functools.partial(gram_kernel, slab, latent_slab),
        "gram",
        (((lax.axis_size("y"), RANK, LANES), f32, True),),
        (shard, pieces),
        1,
        (1,),
    )
    gathered = lax.all_gather(exchange(mine, "y"), "core")
    right, latent_basis, expand_basis = call(
        right_kernel,
        "right",
        (
            ((ring, half, LANES), bf16, True),
            ((RANK, latent_rows), bf16, True),
            ((RANK, expand_rows), bf16, True),
        ),
        (gathered, latent_merged, expand_merged, own_gain),
        0,
        range(4),
    )
    right = exchange(right, RIGHT_OWNERS)
    (piece,) = call(
        functools.partial(right_sum_kernel, 2 * tiles),
        "right_sum",
        (((cross, half, LANES), bf16, True),),
        (place, right),
        1,
        (1,),
    )
    pieces = exchange(piece, RIGHT_CROSS).reshape(shards, depth, half, LANES)
    (mine,) = call(
        functools.partial(factor_kernel, 2 * tiles, latent_tiles, tiles, ring * depth),
        "factor",
        (((ring, half, LANES), bf16, True),),
        (place, shard, pieces),
        2,
        (2,),
    )
    factors = exchange(mine, RIGHT_OWNERS)
    latent_factor, expand_factor = (RANK, latent_cols), (RANK, expand_cols)
    outs = call(
        finish_kernel,
        "finish",
        (
            ((1, *latent_shape), bf16, False),
            (latent_shape, bf16, False),
            (latent_factor, bf16, False),
            ((1, *expand_shape), bf16, False),
            (expand_shape, bf16, False),
            (expand_factor, bf16, False),
            (owned, f32, False),
        ),
        (
            shard,
            factors,
            latent_basis,
            latent_grads,
            latent_errors,
            latent_moments,
            expand_basis,
            expand_grads,
            expand_errors,
            expand_moments,
            gain_before,
        ),
        scalars=1,
        fast=range(1, 11),
        scratch=(
            pltpu.VMEM(latent_shape, bf16),
            pltpu.VMEM(latent_shape, bf16),
            pltpu.VMEM(latent_factor, bf16),
            pltpu.VMEM(expand_shape, bf16),
            pltpu.VMEM(expand_shape, bf16),
            pltpu.VMEM(expand_factor, bf16),
            pltpu.VMEM(owned, f32),
            pltpu.SemaphoreType.DMA((3 + 2 * (len(EXPAND_CUTS) + len(LATENT_CUTS) - 2),)),
        ),
    )
    return (*outs[:2], outs[2].T, *outs[3:5], outs[5].T, outs[6].reshape(-1))


def solution(mesh):
    grid = Mesh(mesh.devices.reshape(8, 8, 2, 4), ("z", "y", "core", "x"))
    return jax.shard_map(
        local,
        mesh=grid,
        in_specs=(
            P(DP, None, "x"),
            P(DP, None, "x"),
            P(None, "x"),
            P("x", None),
            P(DP, "x", None),
            P(DP, "x", None),
            P("x", None),
            P(),
            P(DP, None),
            P("x"),
        ),
        out_specs=(
            P(DP, None, "x"),
            P(None, "x"),
            P("x", None),
            P(DP, "x", None),
            P("x", None),
            P(),
            P("x"),
        ),
        check_vma=False,
    )
```

```python
import functools

import jax
import jax.numpy as jnp
from jax import lax
from jax.experimental import pallas as pl
from jax.experimental.pallas import tpu as pltpu
from jax.sharding import Mesh, PartitionSpec as P

NS_ITERS = 6
BETA = 0.9
EPSILON = 1e-06
RANK = 32
LANES = 128
EXPAND_CUTS = (0, 128, 512, 896, 1280)
LATENT_CUTS = (0, 288)
LEFT_OWNERS = ("core", "y")
LEFT_CROSS = ("z", "x")
RIGHT_OWNERS = ("core", "z")
RIGHT_CROSS = ("x", "y")
DP = ("z", "y", "core")


def dot(left, right, left_dim, right_dim):
    dims = (((left_dim,), (right_dim,)), ((), ()))
    return lax.dot_general(left, right, dims, preferred_element_type=jnp.float32)


def split(whole):
    high = whole.astype(jnp.bfloat16)
    return high, (whole - high.astype(jnp.float32)).astype(jnp.bfloat16)


def fine_dot(left, right, left_dim, right_dim):
    (lh, ll), (rh, rl) = split(left), split(right)
    small = dot(lh, rl, left_dim, right_dim) + dot(ll, rh, left_dim, right_dim)
    return dot(lh, rh, left_dim, right_dim) + small


def inverse_roots(grams):
    row = lax.broadcasted_iota(jnp.int32, (RANK, RANK), 0)
    column = lax.broadcasted_iota(jnp.int32, (RANK, RANK), 1)
    identity = jnp.where(row == column, jnp.float32(1), jnp.float32(0))
    traces = [jnp.sum(g * identity, keepdims=True) + EPSILON for g in grams]
    lefts = [g / t for g, t in zip(grams, traces)]
    middles = [1.5 * identity - 0.5 * y for y in lefts]
    rights = middles
    for repeat_index in range(1, NS_ITERS):
        lefts = [fine_dot(y, m, 1, 0) for y, m in zip(lefts, middles)]
        middles = [
            1.5 * identity - 0.5 * fine_dot(z, y, 1, 0) for z, y in zip(rights, lefts)
        ]
        rights = [fine_dot(m, z, 1, 0) for m, z in zip(middles, rights)]
    return [z / jnp.sqrt(t) for z, t in zip(rights, traces)]


def add(left, right):
    return left.astype(jnp.float32) + right.astype(jnp.float32)


def left_kernel(lg, le, lc, eg, ee, ec, gg, gm, part, lm, em, ggv, gmv, lgv, lev, lcv, egv, eev, ecv, sems):
    ring = part.shape[0]
    slab = em.shape[0] // ring
    latent_slab = lm.shape[0] // ring
    copies = []

    def fetch(source, target):
        copies.append(pltpu.make_async_copy(source, target, sems.at[len(copies)]))
        copies[-1].start()

    fetch(lc, lcv)
    fetch(lg.at[0], lgv)
    fetch(le.at[0], lev)
    fetch(ec, ecv)
    fetch(eg.at[0], egv)
    fetch(ee.at[0], eev)
    fetch(gg, ggv)
    fetch(gm, gmv)
    for c in range(3):
        copies[c].wait()
    lm[...] = add(lgv[...], lev[...]).astype(jnp.bfloat16)
    latent = dot(lcv[...], lm[...], 1, 1)
    rest = jnp.zeros((RANK, LANES - slab - latent_slab), jnp.float32)
    for copy in copies[3:]:
        copy.wait()
    em[...] = add(egv[...], eev[...]).astype(jnp.bfloat16)
    for p in range(ring):
        expand = dot(ecv[...], em[pl.ds(p * slab, slab), :], 1, 1)
        own = latent[:, p * latent_slab : (p + 1) * latent_slab]
        part[p] = jnp.concatenate([expand, own, rest], axis=1).astype(jnp.bfloat16)


def total(parts):
    whole = parts[0].astype(jnp.float32)
    for p in range(1, parts.shape[0]):
        whole = whole + parts[p].astype(jnp.float32)
    return whole


def sum_kernel(parts, out):
    piece = total(parts).astype(out.dtype)
    for p in range(out.shape[0]):
        out[p] = piece


def gram_kernel(slab, latent_slab, shard, pieces, out):
    depth, shards = pieces.shape[:2]
    half = RANK // 2
    gram = jnp.zeros((RANK, RANK), jnp.float32)
    every = jnp.zeros((RANK, LANES), jnp.float32)
    own = jnp.zeros((RANK, LANES), jnp.float32)
    for x in range(shards):
        piece = total(pieces.at[:, x])
        expand = piece[:, :slab]
        gram = gram + fine_dot(expand, expand, 1, 1)
        every = every + piece
        own = jnp.where(shard[0] == x, piece, own)
    lower = gram[half:, half:]
    corner = jnp.concatenate([lower[:, : half // 2], lower[:, half // 2 :]], axis=0)
    used = slab + latent_slab
    rest = jnp.zeros((RANK, LANES - used - half - half // 2), jnp.float32)
    mine = jnp.concatenate(
        [own[:, :slab], every[:, slab:used], gram[:, :half], corner, rest], axis=1
    )
    for p in range(out.shape[0]):
        out[p] = mine


def right_kernel(gathered, lm, em, gain, right, lb, eb):
    cores, line = gathered.shape[:2]
    ring = cores * line
    slab = em.shape[0] // ring
    used = slab + lm.shape[0] // ring
    half = RANK // 2
    places = [(p // line, p % line) for p in range(ring)]
    left = jnp.concatenate([gathered[c, y, :, slab:used] for c, y in places], axis=1)
    latent_gram = fine_dot(left, left, 1, 1)
    packed = total(gathered.at[0])
    for c in range(1, cores):
        packed = packed + total(gathered.at[c])
    first = packed[:, used : used + half]
    corner = packed[:, used + half : used + half + half // 2]
    corner = jnp.concatenate([corner[:half], corner[half:]], axis=1)
    second = jnp.concatenate([first[half:].T, corner], axis=0)
    expand_gram = jnp.concatenate([first, second], axis=1)
    latent_root, expand_root = inverse_roots([latent_gram, expand_gram])
    lb[...] = fine_dot(latent_root, left, 0, 0).astype(jnp.bfloat16)
    left = jnp.concatenate([gathered[c, y, :, :slab] for c, y in places], axis=1)
    eb[...] = fine_dot(expand_root, left, 0, 0).astype(jnp.bfloat16)
    tiles = [
        dot(lb[...], lm[...], 1, 0).astype(jnp.bfloat16),
        dot(eb[...], em[...], 1, 0).astype(jnp.bfloat16),
    ]
    p = 0
    for rows in range(0, RANK, half):
        for tile in tiles:
            for at in range(0, tile.shape[1], LANES):
                right[p] = tile[rows : rows + half, at : at + LANES]
                p += 1
    gains = [gain[:, at : at + LANES].astype(jnp.float32) for at in range(0, gain.shape[1], LANES)]
    gains.append(jnp.zeros((half - len(gains), LANES), jnp.float32))
    right[p] = jnp.concatenate(gains, axis=0).astype(jnp.bfloat16)
    for p in range(p + 1, ring):
        right[p] = jnp.zeros(right.shape[1:], right.dtype)


def halves(whole, is_gain):
    high = whole.astype(jnp.bfloat16).astype(jnp.float32)
    low = whole - high
    row = lax.broadcasted_iota(jnp.int32, whole.shape, 0)
    low = jnp.concatenate([low[:2], low[:2], low[4:]], axis=0)
    spare = jnp.logical_and(is_gain, jnp.logical_and(row >= 2, row < 4))
    return jnp.where(spare, low, high).astype(jnp.bfloat16)


def right_sum_kernel(gain_tile, ring, parts, out):
    piece = halves(total(parts), ring[0] == gain_tile)
    for p in range(out.shape[0]):
        out[p] = piece


def factor_kernel(gain_tile, latent_tiles, tiles, replicas, ring, shard, pieces, out):
    shards, depth = pieces.shape[:2]
    is_gain = ring[0] == gain_tile
    crossed = jnp.logical_and(ring[0] < gain_tile, lax.rem(ring[0], tiles) >= latent_tiles)
    whole = jnp.zeros(pieces.shape[2:], jnp.float32)
    for x in range(shards):
        piece = total(pieces.at[x])
        whole = whole + jnp.where(jnp.logical_or(crossed, shard[0] == x), piece, 0.0)
    whole = whole / replicas
    joined = jnp.concatenate([whole[:2] + whole[2:4], whole[2:]], axis=0)
    piece = halves(jnp.where(is_gain, joined, whole), is_gain)
    for p in range(out.shape[0]):
        out[p] = piece


def finish_kernel(shard, factors, lb, lg, le, lv, eb, eg, ee, ev, gv, *refs):
    ll, lmom, lf, el, emom, ef, gmom = refs[:7]
    llv, lmv, lfv, elv, emv, efv, gmv, sems = refs[7:]
    half = RANK // 2
    tiles = (lf.shape[1] + ef.shape[1]) // LANES
    copies = []

    def send(source, target):
        copies.append(pltpu.make_async_copy(source, target, sems.at[len(copies)]))
        copies[-1].start()

    first = 0
    for factor, out in ((lfv, lf), (efv, ef)):
        count = factor.shape[1] // LANES
        for t in range(count):
            for upper in range(2):
                factor[half * upper : half * (upper + 1), LANES * t : LANES * (t + 1)] = factors[
                    upper * tiles + first + t
                ]
        first += count
        send(factor, out)
    for basis, factor, grads, errors, moments, kept, leftover, fresh, momentum, cuts in (
        (eb, efv, eg, ee, ev, elv, el, emv, emom, EXPAND_CUTS),
        (lb, lfv, lg, le, lv, llv, ll, lmv, lmom, LATENT_CUTS),
    ):
        for low, high in zip(cuts, cuts[1:]):
            rows = pl.ds(low, high - low)
            approx = dot(basis[:, low:high], factor[...], 0, 0)
            whole = add(grads[0, rows, :], errors[0, rows, :])
            kept[rows, :] = (whole - approx).astype(jnp.bfloat16)
            send(kept.at[rows], leftover.at[0, rows])
            fresh[rows, :] = (BETA * moments[rows, :].astype(jnp.float32) + approx).astype(jnp.bfloat16)
            send(fresh.at[rows], momentum.at[rows])
    gain = factors[2 * tiles].astype(jnp.float32)
    gain = gain[:2] + gain[2:4]
    owned = gv.shape[1]
    mean = jnp.zeros((1, owned), jnp.float32)
    for x in range(2 * LANES // owned):
        at = x * owned
        own = gain[at // LANES : at // LANES + 1, at % LANES : at % LANES + owned]
        mean = jnp.where(shard[0] == x, own, mean)
    gmv[...] = BETA * gv[...] + mean
    send(gmv, gmom)
    for copy in copies:
        copy.wait()


def call(kernel, name, outs, args, scalars=0, fast=(), slow=(), scratch=()):
    args = list(args)
    specs = [pl.BlockSpec(memory_space=pltpu.SMEM)] * scalars
    for i in range(scalars, len(args)):
        space = pltpu.HBM if i in slow else pltpu.VMEM
        specs.append(pl.BlockSpec(memory_space=space))
        if i in slow or i in fast:
            args[i] = pltpu.with_memory_space_constraint(args[i], space)
    shapes = [
        pltpu.VMEM(shape, dtype) if near else jax.ShapeDtypeStruct(shape, dtype)
        for shape, dtype, near in outs
    ]
    return pl.pallas_call(
        kernel,
        out_shape=shapes,
        in_specs=specs,
        out_specs=[pl.BlockSpec(memory_space=pltpu.VMEM if near else pl.ANY) for *_, near in outs],
        scratch_shapes=scratch,
        compiler_params=pltpu.CompilerParams(vmem_limit_bytes=16 << 20),
        name=name,
    )(*args)


def exchange(array, axes):
    return lax.all_to_all(array, axes, 0, 0)


def local(
    latent_grads,
    latent_errors,
    latent_moments,
    latent_coeffs,
    expand_grads,
    expand_errors,
    expand_moments,
    expand_coeffs,
    gain_grads,
    gain_moments,
):
    ring = lax.axis_size(LEFT_OWNERS)
    depth = lax.axis_size("z")
    shards = lax.axis_size("x")
    cross = depth * shards
    shard = lax.axis_index("x").astype(jnp.int32).reshape(1)
    place = lax.axis_index(RIGHT_OWNERS).astype(jnp.int32).reshape(1)
    latent_rows, latent_cols = latent_grads.shape[1:]
    expand_rows, expand_cols = expand_grads.shape[1:]
    slab = expand_rows // ring
    latent_slab = latent_rows // ring
    latent_tiles = latent_cols // LANES
    tiles = latent_tiles + expand_cols // LANES
    half = RANK // 2
    bf16, f32 = jnp.bfloat16, jnp.float32

    latent_shape, expand_shape = (latent_rows, latent_cols), (expand_rows, expand_cols)
    owned = (1, gain_moments.shape[0])
    part, latent_merged, expand_merged, own_gain, gain_before = call(
        left_kernel,
        "left",
        (
            ((ring, RANK, LANES), bf16, True),
            (latent_shape, bf16, True),
            (expand_shape, bf16, True),
            (gain_grads.shape, bf16, True),
            (owned, f32, True),
        ),
        (
            latent_grads,
            latent_errors,
            latent_coeffs.T,
            expand_grads,
            expand_errors,
            expand_coeffs.T,
            gain_grads,
            gain_moments.reshape(owned),
        ),
        slow=range(8),
        scratch=(
            pltpu.VMEM(latent_shape, bf16),
            pltpu.VMEM(latent_shape, bf16),
            pltpu.VMEM((RANK, latent_cols), bf16),
            pltpu.VMEM(expand_shape, bf16),
            pltpu.VMEM(expand_shape, bf16),
            pltpu.VMEM((RANK, expand_cols), bf16),
            pltpu.SemaphoreType.DMA((8,)),
        ),
    )
    part, shard, place = lax.optimization_barrier((part, shard, place))
    part = exchange(part, LEFT_OWNERS)
    (piece,) = call(sum_kernel, "left_sum", (((cross, RANK, LANES), bf16, True),), (part,), 0, (0,))
    pieces = exchange(piece, LEFT_CROSS).reshape(depth, shards, RANK, LANES)
    (mine,) = call(
        functools.partial(gram_kernel, slab, latent_slab),
        "gram",
        (((lax.axis_size("y"), RANK, LANES), f32, True),),
        (shard, pieces),
        1,
        (1,),
    )
    gathered = lax.all_gather(exchange(mine, "y"), "core")
    right, latent_basis, expand_basis = call(
        right_kernel,
        "right",
        (
            ((ring, half, LANES), bf16, True),
            ((RANK, latent_rows), bf16, True),
            ((RANK, expand_rows), bf16, True),
        ),
        (gathered, latent_merged, expand_merged, own_gain),
        0,
        range(4),
    )
    right = exchange(right, RIGHT_OWNERS)
    (piece,) = call(
        functools.partial(right_sum_kernel, 2 * tiles),
        "right_sum",
        (((cross, half, LANES), bf16, True),),
        (place, right),
        1,
        (1,),
    )
    pieces = exchange(piece, RIGHT_CROSS).reshape(shards, depth, half, LANES)
    (mine,) = call(
        functools.partial(factor_kernel, 2 * tiles, latent_tiles, tiles, ring * depth),
        "factor",
        (((ring, half, LANES), bf16, True),),
        (place, shard, pieces),
        2,
        (2,),
    )
    factors = exchange(mine, RIGHT_OWNERS)
    latent_factor, expand_factor = (RANK, latent_cols), (RANK, expand_cols)
    outs = call(
        finish_kernel,
        "finish",
        (
            ((1, *latent_shape), bf16, False),
            (latent_shape, bf16, False),
            (latent_factor, bf16, False),
            ((1, *expand_shape), bf16, False),
            (expand_shape, bf16, False),
            (expand_factor, bf16, False),
            (owned, f32, False),
        ),
        (
            shard,
            factors,
            latent_basis,
            latent_grads,
            latent_errors,
            latent_moments,
            expand_basis,
            expand_grads,
            expand_errors,
            expand_moments,
            gain_before,
        ),
        scalars=1,
        fast=range(1, 11),
        scratch=(
            pltpu.VMEM(latent_shape, bf16),
            pltpu.VMEM(latent_shape, bf16),
            pltpu.VMEM(latent_factor, bf16),
            pltpu.VMEM(expand_shape, bf16),
            pltpu.VMEM(expand_shape, bf16),
            pltpu.VMEM(expand_factor, bf16),
            pltpu.VMEM(owned, f32),
            pltpu.SemaphoreType.DMA((3 + 2 * (len(EXPAND_CUTS) + len(LATENT_CUTS) - 2),)),
        ),
    )
    return (*outs[:2], outs[2].T, *outs[3:5], outs[5].T, outs[6].reshape(-1))


def solution(mesh):
    grid = Mesh(mesh.devices.reshape(8, 8, 2, 4), ("z", "y", "core", "x"))
    return jax.shard_map(
        local,
        mesh=grid,
        in_specs=(
            P(DP, None, "x"),
            P(DP, None, "x"),
            P(None, "x"),
            P("x", None),
            P(DP, "x", None),
            P(DP, "x", None),
            P("x", None),
            P(),
            P(DP, None),
            P("x"),
        ),
        out_specs=(
            P(DP, None, "x"),
            P(None, "x"),
            P("x", None),
            P(DP, "x", None),
            P("x", None),
            P(),
            P("x"),
        ),
        check_vma=False,
    )
```
